32 devices in a mesh: ctx: 8 (over z, x), ch: 4 (over y, core).
Axes of the slice: x: 2, y: 2, z: 4, core: 2. Of those that a mesh axis runs over, the one named last changes fastest.
Arguments:
- tokens: bfloat16 [2048, 4096], P('ctx', 'ch'), may hold values from -6 to 6
- in_weight: bfloat16 [4096, 3, 4096], P('ch', None, 'ctx'), may hold values from -0.09375 to 0.09375
- short_filter: float32 [4096, 3, 3], P('ch'), may hold values from -3 to 3
- decay_rates: float32 [4096, 16], P('ch'), may hold values from 0.00024414062 to 0.05
- residues: float32 [4096, 16], P('ch'), may hold values from -1.5 to 1.5
- skip_gain: float32 [4096], P('ch'), may hold values from -4 to 4
- out_weight: bfloat16 [4096, 4096], P(None, 'ch'), may hold values from -0.09375 to 0.09375
Outputs:
- mixed: bfloat16 [2048, 4096], P('ctx', 'ch')
The draws below stay inside these ranges and needn't reach their ends.
All inputs are finite; a program needn't handle non-finite values.
Results may differ from the reference program's by a relative error of at most 0.02.
Values may be sent and summed in bfloat16 or wider, within the bound.
A program may use at most 320 MiB of HBM per device.

```python
import math
import jax
import jax.numpy as jnp

D = 4096
C = 4096
ORDER = 16
SHORT = 3
SEQ_LEN = 2048
N_CH = 4


def steps_of(own_key, extent, split, least, top_value):
    level = 1.0
    for dim, blocks in split:
        heights = jax.random.uniform(jax.random.fold_in(jax.random.fold_in(own_key, 6), dim), (blocks,), jnp.float32, least / len(split), top_value / len(split))
        level = level * jnp.repeat(jnp.exp(heights), extent[dim] // blocks).reshape((-1,) + (1,) * (len(extent) - 1 - dim))
    return level


def gaussian(rng, dims, scale, reach, pieces=(), held_as=jnp.bfloat16):
    array = scale * jax.random.normal(rng, dims, jnp.float32)
    if pieces:
        array = array * steps_of(rng, dims, pieces, -0.22, 0.18)
    return jnp.clip(array, -reach, reach).astype(held_as)


def setup_inputs(seed: int = 0) -> dict:
    key_of = jax.random.split(jax.random.key(seed), 8)
    return {
        "tokens": gaussian(key_of[0], (SEQ_LEN, D), 1.0, 6.0, ((0, 8), (1, 4))),
        "in_weight": gaussian(key_of[1], (D, 3, C), D ** -0.5, 0.09375, ((0, 4), (2, 8))),
        "short_filter": gaussian(key_of[2], (C, 3, SHORT), 0.6, 3.0, ((0, 4),), jnp.float32),
        "decay_rates": jnp.clip(jnp.exp(math.log(0.05) - 5.322034 * jax.random.uniform(key_of[3], (C, ORDER), jnp.float32) ** steps_of(key_of[3], (C, ORDER), ((0, 4),), -0.2, 0.2)), 0.00024414062, 0.05),
        "residues": gaussian(key_of[4], (C, ORDER), 0.25, 1.5, ((0, 4),), jnp.float32),
        "skip_gain": gaussian(key_of[5], (C,), 1.0, 4.0, ((0, 4),), jnp.float32),
        "out_weight": gaussian(key_of[6], (C, D), C ** -0.5, 0.09375, ((1, 4),)),
    }


def reference(tokens, in_weight, short_filter, decay_rates, residues, skip_gain, out_weight):
    width = D // N_CH
    flat_weight = in_weight.reshape(D, 3 * C)
    summed = jnp.zeros((SEQ_LEN, 3 * C), jnp.float32)
    for group_index in range(N_CH):
        part_tokens = tokens[:, group_index * width:(group_index + 1) * width]
        part_weight = flat_weight[group_index * width:(group_index + 1) * width]
        partial_value = jnp.dot(part_tokens, part_weight, preferred_element_type=jnp.float32).astype(jnp.bfloat16)
        summed = summed + partial_value.astype(jnp.float32)
    projected = summed.reshape(SEQ_LEN, 3, C).astype(jnp.bfloat16).astype(jnp.float32)
    padded = jnp.pad(projected, ((SHORT - 1, 0), (0, 0), (0, 0)))
    taps = jnp.transpose(short_filter, (2, 1, 0))
    featured = jnp.zeros((SEQ_LEN, 3, C), jnp.float32)
    for shift_by in range(SHORT):
        begin = SHORT - 1 - shift_by
        featured = featured + taps[shift_by][None] * padded[begin:begin + SEQ_LEN]
    query = featured[:, 0]
    product = (featured[:, 1] * featured[:, 2]).astype(jnp.bfloat16)
    steps_axis = jnp.arange(SEQ_LEN).astype(jnp.float32)
    mode_gain = residues * jnp.sqrt(-jnp.expm1(-2.0 * decay_rates))
    long_filter = jnp.zeros((C, SEQ_LEN), jnp.float32)
    for mode in range(ORDER):
        long_filter = long_filter + mode_gain[:, mode:mode + 1] * jnp.exp(-decay_rates[:, mode:mode + 1] * steps_axis[None])
    length = 2 * SEQ_LEN
    spectrum = jnp.fft.rfft(product.astype(jnp.float32), n=length, axis=0) * jnp.fft.rfft(long_filter.T, n=length, axis=0)
    convolved = jnp.fft.irfft(spectrum, n=length, axis=0)[:SEQ_LEN]
    gated = (query * (convolved + skip_gain[None] * product.astype(jnp.float32))).astype(jnp.bfloat16)
    return jnp.dot(gated, out_weight, preferred_element_type=jnp.float32).astype(jnp.bfloat16)
```

```python
import functools

import jax
import jax.numpy as jnp
from jax import lax
from jax.experimental import pallas as pl
from jax.experimental.pallas import tpu as pltpu
from jax.sharding import PartitionSpec as P

LANES = 8


def conv_kernel(x_ref, taps_ref, decay_ref, gain_ref, skip_ref, out_ref, xs, ps, qs):
    _, length, chans = x_ref.shape
    modes = decay_ref.shape[0]
    reach = taps_ref.shape[1] - 1
    run = length // LANES
    rows = 256 if length % 256 == 0 else length

    def widen(k, _):
        at = pl.ds(pl.multiple_of(k * rows, rows), rows)
        for s in range(3):
            xs[s, at, :] = x_ref[s, at, :].astype(jnp.float32)
        return 0

    lax.fori_loop(0, length // rows, widen, 0)

    def wide(row):
        return jnp.broadcast_to(row, (LANES, chans))

    first = lax.broadcasted_iota(jnp.int32, (LANES, chans), 0) == 0
    rates = [decay_ref[n : n + 1, :] for n in range(modes)]
    a = [wide(jnp.exp(-r)) for r in rates]
    taps = [[wide(taps_ref[s, j : j + 1, :]) for j in range(reach + 1)] for s in range(3)]
    zero = jnp.zeros((LANES, chans), jnp.float32)

    def column(ref, t):
        return ref[pl.ds(t, LANES, stride=run), :]

    before = []
    for s in range(3):
        for j in range(1, reach + 1):
            last = column(xs.at[s], run - j)
            before.append(jnp.where(first, 0.0, pltpu.roll(last, 1, 0)))

    def sweep(t, carry):
        past, states = carry
        feats, now = [], []
        for s in range(3):
            x = column(xs.at[s], t)
            mine = past[s * reach : (s + 1) * reach]
            f = taps[s][0] * x
            for j in range(reach):
                f = f + taps[s][j + 1] * mine[j]
            feats.append(f)
            now += [x] + list(mine[: reach - 1])
        p = (feats[1] * feats[2]).astype(jnp.bfloat16).astype(jnp.float32)
        qs[pl.ds(t, LANES, stride=run), :] = feats[0]
        ps[pl.ds(t, LANES, stride=run), :] = p
        return tuple(now), tuple(a[n] * states[n] + p for n in range(modes))

    _, ends = lax.fori_loop(0, run, sweep, (tuple(before), (zero,) * modes), unroll=2)

    starts = []
    for n in range(modes):
        through = wide(jnp.exp(-rates[n] * float(run)))
        state = zero
        for _ in range(LANES - 1):
            state = jnp.where(first, 0.0, pltpu.roll(through * state + ends[n], 1, 0))
        starts.append(state)

    gain = [wide(gain_ref[n : n + 1, :]) for n in range(modes)]
    skip = wide(skip_ref[...])

    def emit(t, states):
        p = column(ps, t)
        states = tuple(a[n] * states[n] + p for n in range(modes))
        terms = [gain[n] * states[n] for n in range(modes)] + [skip * p]
        while len(terms) > 1:
            terms = [sum(terms[k : k + 2][1:], terms[k]) for k in range(0, len(terms), 2)]
        at = pl.ds(t, LANES, stride=run)
        qs[at, :] = qs[at, :] * terms[0]
        return states

    lax.fori_loop(0, run, emit, tuple(starts), unroll=2)

    def narrow(k, _):
        at = pl.ds(pl.multiple_of(k * rows, rows), rows)
        out_ref[at, :] = qs[at, :].astype(jnp.bfloat16)
        return 0

    lax.fori_loop(0, length // rows, narrow, 0)


def convolve(projected, taps, decay, gain, skip):
    _, length, chans = projected.shape
    return pl.pallas_call(
        conv_kernel,
        out_shape=jax.ShapeDtypeStruct((length, chans), jnp.bfloat16),
        in_specs=[pl.BlockSpec(memory_space=pltpu.VMEM)] * 5,
        out_specs=pl.BlockSpec(memory_space=pltpu.VMEM),
        scratch_shapes=[
            pltpu.VMEM((3, length, chans), jnp.float32),
            pltpu.VMEM((length, chans), jnp.float32),
            pltpu.VMEM((length, chans), jnp.float32),
        ],
        compiler_params=pltpu.CompilerParams(vmem_limit_bytes=60 << 20),
    )(projected, taps, decay, gain, skip)


def own_parameters(short_filter, decay_rates, residues, skip_gain, chans):
    n_ctx, n_ch = lax.axis_size("ctx"), lax.axis_size("ch")
    start = lax.axis_index("ctx") * chans
    flat = short_filter.reshape(short_filter.shape[0], -1)
    packed = jnp.concatenate([flat, decay_rates, residues, skip_gain[:, None]], axis=1)
    piece = lax.dynamic_slice_in_dim(packed, start, chans, 0)
    pairs = []
    for s in range(n_ctx):
        for c in range(n_ch):
            pairs.append((s * n_ch + c, c * n_ctx + s))
    mine = lax.ppermute(piece, ("ctx", "ch"), pairs).T
    n_taps, order = flat.shape[1], decay_rates.shape[1]
    taps = mine[:n_taps].reshape(short_filter.shape[1], short_filter.shape[2], chans)
    decay = mine[n_taps : n_taps + order]
    gain = mine[n_taps + order : n_taps + 2 * order] * jnp.sqrt(-jnp.expm1(-2.0 * decay))
    return taps, decay, gain, mine[n_taps + 2 * order :]


def local(tokens, in_weight, short_filter, decay_rates, residues, skip_gain, out_weight):
    n_ctx, n_ch = lax.axis_size("ctx"), lax.axis_size("ch")
    rows_here = tokens.shape[0]
    chans = in_weight.shape[2] // n_ch
    taps, decay, gain, skip = own_parameters(short_filter, decay_rates, residues, skip_gain, chans)
    everyone = lax.all_gather(tokens, "ctx", axis=0, tiled=True)
    terms = jnp.einsum("rd,dsc->src", everyone, in_weight, preferred_element_type=jnp.float32)
    projected = lax.psum_scatter(terms.astype(jnp.bfloat16), "ch", scatter_dimension=2, tiled=True)
    gated = convolve(projected, taps, decay, gain, skip)
    sent = gated.reshape(n_ctx, rows_here, chans)
    mine = lax.all_to_all(sent, "ctx", split_axis=0, concat_axis=0, tiled=True)
    every = lax.all_gather(mine, "ch", axis=0)
    weight = out_weight.reshape(n_ctx, n_ch, chans, out_weight.shape[1])
    mixed = jnp.einsum("jirc,ijcd->rd", every, weight, preferred_element_type=jnp.float32)
    return mixed.astype(jnp.bfloat16)


def solution(mesh):
    in_specs = (
        P("ctx", "ch"),
        P("ch", None, "ctx"),
        P("ch", None, None),
        P("ch", None),
        P("ch", None),
        P("ch"),
        P(None, "ch"),
    )
    out_specs = P("ctx", "ch")
    return jax.shard_map(local, mesh=mesh, in_specs=in_specs, out_specs=out_specs, check_vma=False)
```

```python
import functools

import jax
import jax.numpy as jnp
from jax import lax
from jax.experimental import pallas as pl
from jax.experimental.pallas import tpu as pltpu
from jax.sharding import PartitionSpec as P

LANES = 8


def conv_kernel(x_ref, taps_ref, decay_ref, gain_ref, skip_ref, out_ref, xs, ps, qs):
    _, length, chans = x_ref.shape
    modes = decay_ref.shape[0]
    reach = taps_ref.shape[1] - 1
    run = length // LANES
    rows = 256 if length % 256 == 0 else length

    def widen(k, _):
        at = pl.ds(pl.multiple_of(k * rows, rows), rows)
        for s in range(3):
            xs[s, at, :] = x_ref[s, at, :].astype(jnp.float32)
        return 0

    lax.fori_loop(0, length // rows, widen, 0)

    def wide(row):
        return jnp.broadcast_to(row, (LANES, chans))

    first = lax.broadcasted_iota(jnp.int32, (LANES, chans), 0) == 0
    rates = [decay_ref[n : n + 1, :] for n in range(modes)]
    a = [wide(jnp.exp(-r)) for r in rates]
    taps = [[wide(taps_ref[s, j : j + 1, :]) for j in range(reach + 1)] for s in range(3)]
    zero = jnp.zeros((LANES, chans), jnp.float32)

    def column(ref, t):
        return ref[pl.ds(t, LANES, stride=run), :]

    before = []
    for s in range(3):
        for j in range(1, reach + 1):
            last = column(xs.at[s], run - j)
            before.append(jnp.where(first, 0.0, pltpu.roll(last, 1, 0)))

    def sweep(t, carry):
        past, states = carry
        feats, now = [], []
        for s in range(3):
            x = column(xs.at[s], t)
            mine = past[s * reach : (s + 1) * reach]
            f = taps[s][0] * x
            for j in range(reach):
                f = f + taps[s][j + 1] * mine[j]
            feats.append(f)
            now += [x] + list(mine[: reach - 1])
        p = (feats[1] * feats[2]).astype(jnp.bfloat16).astype(jnp.float32)
        qs[pl.ds(t, LANES, stride=run), :] = feats[0]
        ps[pl.ds(t, LANES, stride=run), :] = p
        return tuple(now), tuple(a[n] * states[n] + p for n in range(modes))

    _, ends = lax.fori_loop(0, run, sweep, (tuple(before), (zero,) * modes), unroll=2)

    starts = []
    for n in range(modes):
        through = wide(jnp.exp(-rates[n] * float(run)))
        state = zero
        for _ in range(LANES - 1):
            state = jnp.where(first, 0.0, pltpu.roll(through * state + ends[n], 1, 0))
        starts.append(state)

    gain = [wide(gain_ref[n : n + 1, :]) for n in range(modes)]
    skip = wide(skip_ref[...])

    def emit(t, states):
        p = column(ps, t)
        states = tuple(a[n] * states[n] + p for n in range(modes))
        terms = [gain[n] * states[n] for n in range(modes)] + [skip * p]
        while len(terms) > 1:
            terms = [sum(terms[k : k + 2][1:], terms[k]) for k in range(0, len(terms), 2)]
        at = pl.ds(t, LANES, stride=run)
        qs[at, :] = qs[at, :] * terms[0]
        return states

    lax.fori_loop(0, run, emit, tuple(starts), unroll=2)

    def narrow(k, _):
        at = pl.ds(pl.multiple_of(k * rows, rows), rows)
        out_ref[at, :] = qs[at, :].astype(jnp.bfloat16)
        return 0

    lax.fori_loop(0, length // rows, narrow, 0)


def convolve(projected, taps, decay, gain, skip):
    _, length, chans = projected.shape
    return pl.pallas_call(
        conv_kernel,
        out_shape=jax.ShapeDtypeStruct((length, chans), jnp.bfloat16),
        in_specs=[pl.BlockSpec(memory_space=pltpu.VMEM)] * 5,
        out_specs=pl.BlockSpec(memory_space=pltpu.VMEM),
        scratch_shapes=[
            pltpu.VMEM((3, length, chans), jnp.float32),
            pltpu.VMEM((length, chans), jnp.float32),
            pltpu.VMEM((length, chans), jnp.float32),
        ],
        compiler_params=pltpu.CompilerParams(vmem_limit_bytes=60 << 20),
    )(projected, taps, decay, gain, skip)


MESH = pl.DeviceIdType.MESH


def remote(src, dst, send, recv, device):
    return pltpu.make_async_remote_copy(
        src_ref=src, dst_ref=dst, send_sem=send, recv_sem=recv, device_id=device, device_id_type=MESH
    )


def project_kernel(
    n_ctx, tok_ref, w_hbm, out_ref, held, w, part, near, sums, far,
    w_sem, up_s, down_s, line_r, pair_s, pair_r, near_s, near_r, far_s, far_r,
):
    rows = tok_ref.shape[0]
    streams, _, width = w.shape
    chans = width // 4
    line = n_ctx // 2
    ctx, ch = lax.axis_index("ctx"), lax.axis_index("ch")
    z, x = lax.div(ctx, 2), lax.rem(ctx, 2)
    y, core = lax.div(ch, 2), lax.rem(ch, 2)
    near_ch, far_ch = y * 2 + 1 - core, (1 - y) * 2 + core
    has_up, has_down = z + 1 < line, z > 0

    load = pltpu.make_async_copy(w_hbm, w, w_sem)
    load.start()
    held[ctx] = tok_ref[...]

    barrier = pltpu.get_barrier_semaphore()

    def greet(*device):
        pl.semaphore_signal(barrier, inc=1, device_id=device, device_id_type=MESH)

    greet(z * 2 + 1 - x, ch)
    greet(ctx, near_ch)
    greet(ctx, far_ch)

    @pl.when(has_up)
    def _():
        greet(ctx + 2, ch)

    @pl.when(has_down)
    def _():
        greet(ctx - 2, ch)

    pl.semaphore_wait(barrier, 3 + has_up.astype(jnp.int32) + has_down.astype(jnp.int32))

    def up_copy(src):
        at = held.at[src * 2 + x]
        return remote(at, at, up_s.at[src], line_r.at[src], (ctx + 2, ch))

    def down_copy(src):
        at = held.at[src * 2 + x]
        return remote(at, at, down_s.at[src], line_r.at[src], (ctx - 2, ch))

    def pair_copy(src, side):
        at = held.at[src * 2 + side]
        return remote(at, at, pair_s.at[src], pair_r.at[src], (z * 2 + 1 - x, ch))

    def near_copy(r):
        return remote(part.at[1 - core, r], near.at[r], near_s.at[r], near_r.at[r], (ctx, near_ch))

    def far_copy(r):
        return remote(sums.at[r], far.at[r], far_s.at[r], far_r.at[r], (ctx, far_ch))

    @pl.when(has_up)
    def _():
        up_copy(z).start()

    @pl.when(has_down)
    def _():
        down_copy(z).start()

    pair_copy(z, x).start()
    load.wait()

    def compute(r):
        def stream(s, _):
            for half in range(2):
                acc = jnp.dot(
                    held[r],
                    w[s, :, half * 2 * chans : (half + 1) * 2 * chans],
                    preferred_element_type=jnp.float32,
                ).astype(jnp.bfloat16)
                part[0, r, half, s] = acc[:, :chans]
                part[1, r, half, s] = acc[:, chans:]
            return 0

        lax.fori_loop(0, streams, stream, 0)
        near_copy(r).start()

    def combine(r):
        near_copy(r).wait_recv()
        for s in range(streams):
            both = part[core, r, 1 - y, s].astype(jnp.float32) + near[r, 1 - y, s].astype(jnp.float32)
            sums[r, s] = both.astype(jnp.bfloat16)
        far_copy(r).start()

    def place(s):
        away = lax.div(s + 1, 2)
        sign = 2 * lax.rem(s + 1, 2) - 1
        at = z + away * sign
        return at, sign, (s >= 0) & (at >= 0) & (at < line)

    def step(s, _):
        at, sign, valid = place(s)

        @pl.when(valid)
        def _():
            @pl.when(s > 0)
            def _():
                up_copy(at).wait_recv()

                @pl.when((sign < 0) & has_up)
                def _():
                    up_copy(at).start()

                @pl.when((sign > 0) & has_down)
                def _():
                    down_copy(at).start()

                pair_copy(at, x).start()

            compute(at * 2 + x)

        at1, _, valid1 = place(s - 1)

        @pl.when(valid1)
        def _():
            pair_copy(at1, 1 - x).wait_recv()
            compute(at1 * 2 + 1 - x)
            combine(at1 * 2 + x)

        at2, _, valid2 = place(s - 2)

        @pl.when(valid2)
        def _():
            combine(at2 * 2 + 1 - x)

        return 0

    lax.fori_loop(0, 2 * line + 1, step, 0)

    def finish(r, _):
        far_copy(r).wait_recv()
        at = pl.ds(pl.multiple_of(r * rows, rows), rows)
        for s in range(streams):
            total = part[core, r, y, s].astype(jnp.float32) + near[r, y, s].astype(jnp.float32)
            out_ref[s, at, :] = (total + far[r, s].astype(jnp.float32)).astype(jnp.bfloat16)
        return 0

    lax.fori_loop(0, n_ctx, finish, 0)

    def drain(r, _):
        near_copy(r).wait_send()
        far_copy(r).wait_send()
        return 0

    lax.fori_loop(0, n_ctx, drain, 0)

    def drain_line(src, _):
        pair_copy(src, x).wait_send()

        @pl.when(has_up & (src <= z))
        def _():
            up_copy(src).wait_send()

        @pl.when(has_down & (src >= z))
        def _():
            down_copy(src).wait_send()

        return 0

    lax.fori_loop(0, line, drain_line, 0)


def project(tokens, in_weight):
    n_ctx = lax.axis_size("ctx")
    rows, depth = tokens.shape
    streams, width = in_weight.shape[1:]
    chans = width // 4
    dma = pltpu.SemaphoreType.DMA
    line = n_ctx // 2
    return pl.pallas_call(
        functools.partial(project_kernel, n_ctx),
        out_shape=jax.ShapeDtypeStruct((streams, n_ctx * rows, chans), jnp.bfloat16),
        in_specs=[pl.BlockSpec(memory_space=pltpu.VMEM), pl.BlockSpec(memory_space=pl.ANY)],
        out_specs=pl.BlockSpec(memory_space=pltpu.VMEM),
        scratch_shapes=[
            pltpu.VMEM((n_ctx, rows, depth), jnp.bfloat16),
            pltpu.VMEM((streams, depth, width), jnp.bfloat16),
            pltpu.VMEM((2, n_ctx, 2, streams, rows, chans), jnp.bfloat16),
            pltpu.VMEM((n_ctx, 2, streams, rows, chans), jnp.bfloat16),
            pltpu.VMEM((n_ctx, streams, rows, chans), jnp.bfloat16),
            pltpu.VMEM((n_ctx, streams, rows, chans), jnp.bfloat16),
            dma,
        ]
        + [dma((line,))] * 5
        + [dma((n_ctx,))] * 4,
        compiler_params=pltpu.CompilerParams(
            collective_id=0, has_side_effects=True, vmem_limit_bytes=48 << 20
        ),
    )(tokens, jnp.transpose(in_weight, (1, 0, 2)))


def mix_kernel(
    n_ctx, g_ref, w_hbm, out_ref, blocks, w, acc,
    w_sem, sent_s, sent_r, far_s, far_r, near_s, near_r, relay_s, relay_r,
):
    chans = g_ref.shape[2]
    width = 4 * chans
    ctx, ch = lax.axis_index("ctx"), lax.axis_index("ch")
    y, core = lax.div(ch, 2), lax.rem(ch, 2)
    near_ch, far_ch, cross_ch = y * 2 + 1 - core, (1 - y) * 2 + core, (1 - y) * 2 + 1 - core
    load = pltpu.make_async_copy(w_hbm, w, w_sem)
    load.start()

    def lanes(j):
        return pl.ds(pl.multiple_of(j * chans, chans), chans)

    def peer(k):
        return lax.rem(ctx + k, n_ctx)

    barrier = pltpu.get_barrier_semaphore()

    def greet(device):
        pl.semaphore_signal(barrier, inc=1, device_id=device, device_id_type=MESH)

    def greet_peer(k, _):
        greet((peer(k), ch))
        return 0

    lax.fori_loop(1, n_ctx, greet_peer, 0)
    greet((ctx, near_ch))
    greet((ctx, far_ch))
    blocks[ctx, :, lanes(ch)] = g_ref[ctx]
    acc[...] = jnp.zeros_like(acc)
    pl.semaphore_wait(barrier, n_ctx + 1)

    def sent_copy(dest):
        return remote(
            g_ref.at[dest], blocks.at[ctx, :, lanes(ch)], sent_s.at[dest], sent_r.at[ctx], (dest, ch)
        )

    def arrival(src):
        at = blocks.at[src, :, lanes(ch)]
        return remote(at, at, sent_s.at[src], sent_r.at[src], (src, ch))

    def far_copy(src, j):
        at = blocks.at[src, :, lanes(j)]
        return remote(at, at, far_s.at[src], far_r.at[src], (ctx, far_ch))

    def near_copy(src, j):
        at = blocks.at[src, :, lanes(j)]
        return remote(at, at, near_s.at[src], near_r.at[src], (ctx, near_ch))

    def relay_copy(src, j):
        at = blocks.at[src, :, lanes(j)]
        return remote(at, at, relay_s.at[src], relay_r.at[src], (ctx, near_ch))

    def send(k, _):
        sent_copy(peer(k)).start()
        return 0

    lax.fori_loop(1, n_ctx, send, 0)

    def step(k, _):
        @pl.when(k < n_ctx)
        def _():
            src = peer(n_ctx - k)

            @pl.when(k > 0)
            def _():
                arrival(src).wait_recv()

            far_copy(src, ch).start()
            near_copy(src, ch).start()

        @pl.when((k >= 1) & (k <= n_ctx))
        def _():
            src = peer(n_ctx - k + 1)
            far_copy(src, far_ch).wait_recv()
            relay_copy(src, far_ch).start()

        @pl.when(k == 1)
        def _():
            load.wait()

        @pl.when(k >= 2)
        def _():
            src = peer(n_ctx - k + 2)
            near_copy(src, near_ch).wait_recv()
            relay_copy(src, cross_ch).wait_recv()
            at = pl.ds(pl.multiple_of(src * width, width), width)
            acc[...] += jnp.dot(blocks[src], w[at, :], preferred_element_type=jnp.float32)

        return 0

    lax.fori_loop(0, n_ctx + 2, step, 0)
    out_ref[...] = acc[...].astype(jnp.bfloat16)

    def drain(k, _):
        src = peer(k)

        @pl.when(k > 0)
        def _():
            sent_copy(src).wait_send()

        far_copy(src, ch).wait_send()
        near_copy(src, ch).wait_send()
        relay_copy(src, far_ch).wait_send()
        return 0

    lax.fori_loop(0, n_ctx, drain, 0)


def mix(gated, out_weight):
    n_ctx, rows, chans = gated.shape
    dma = pltpu.SemaphoreType.DMA
    return pl.pallas_call(
        functools.partial(mix_kernel, n_ctx),
        out_shape=jax.ShapeDtypeStruct((rows, out_weight.shape[1]), jnp.bfloat16),
        in_specs=[pl.BlockSpec(memory_space=pltpu.VMEM), pl.BlockSpec(memory_space=pl.ANY)],
        out_specs=pl.BlockSpec(memory_space=pltpu.VMEM),
        scratch_shapes=[
            pltpu.VMEM((n_ctx, rows, 4 * chans), jnp.bfloat16),
            pltpu.VMEM(out_weight.shape, jnp.bfloat16),
            pltpu.VMEM((rows, out_weight.shape[1]), jnp.float32),
            dma,
        ]
        + [dma((n_ctx,))] * 8,
        compiler_params=pltpu.CompilerParams(
            collective_id=1, has_side_effects=True, vmem_limit_bytes=48 << 20
        ),
    )(gated, out_weight)


def own_parameters(short_filter, decay_rates, residues, skip_gain, chans):
    n_ctx, n_ch = lax.axis_size("ctx"), lax.axis_size("ch")
    start = lax.axis_index("ctx") * chans
    flat = short_filter.reshape(short_filter.shape[0], -1)
    packed = jnp.concatenate([flat, decay_rates, residues, skip_gain[:, None]], axis=1)
    piece = lax.dynamic_slice_in_dim(packed, start, chans, 0)
    pairs = []
    for s in range(n_ctx):
        for c in range(n_ch):
            pairs.append((s * n_ch + c, c * n_ctx + s))
    mine = lax.ppermute(piece, ("ctx", "ch"), pairs).T
    n_taps, order = flat.shape[1], decay_rates.shape[1]
    taps = mine[:n_taps].reshape(short_filter.shape[1], short_filter.shape[2], chans)
    decay = mine[n_taps : n_taps + order]
    gain = mine[n_taps + order : n_taps + 2 * order] * jnp.sqrt(-jnp.expm1(-2.0 * decay))
    return taps, decay, gain, mine[n_taps + 2 * order :]


def local(tokens, in_weight, short_filter, decay_rates, residues, skip_gain, out_weight):
    n_ctx, n_ch = lax.axis_size("ctx"), lax.axis_size("ch")
    rows_here = tokens.shape[0]
    chans = in_weight.shape[2] // n_ch
    taps, decay, gain, skip = own_parameters(short_filter, decay_rates, residues, skip_gain, chans)
    if n_ch == 4 and n_ctx % 2 == 0 and chans % 128 == 0:
        gated = convolve(project(tokens, in_weight), taps, decay, gain, skip)
        return mix(gated.reshape(n_ctx, rows_here, chans), out_weight)
    everyone = lax.all_gather(tokens, "ctx", axis=0, tiled=True)
    terms = jnp.einsum("rd,dsc->src", everyone, in_weight, preferred_element_type=jnp.float32)
    projected = lax.psum_scatter(terms.astype(jnp.bfloat16), "ch", scatter_dimension=2, tiled=True)
    gated = convolve(projected, taps, decay, gain, skip)
    sent = gated.reshape(n_ctx, rows_here, chans)
    mine = lax.all_to_all(sent, "ctx", split_axis=0, concat_axis=0, tiled=True)
    every = lax.all_gather(mine, "ch", axis=0)
    weight = out_weight.reshape(n_ctx, n_ch, chans, out_weight.shape[1])
    mixed = jnp.einsum("jirc,ijcd->rd", every, weight, preferred_element_type=jnp.float32)
    return mixed.astype(jnp.bfloat16)


def solution(mesh):
    in_specs = (
        P("ctx", "ch"),
        P("ch", None, "ctx"),
        P("ch", None, None),
        P("ch", None),
        P("ch", None),
        P("ch"),
        P(None, "ch"),
    )
    out_specs = P("ctx", "ch")
    return jax.shard_map(local, mesh=mesh, in_specs=in_specs, out_specs=out_specs, check_vma=False)
```

```python
import functools

import jax
import jax.numpy as jnp
from jax import lax
from jax.experimental import pallas as pl
from jax.experimental.pallas import tpu as pltpu
from jax.sharding import PartitionSpec as P

LANES = 8


def conv_kernel(x_ref, taps_ref, decay_ref, gain_ref, skip_ref, out_ref, xs, ps, qs):
    _, length, chans = x_ref.shape
    modes = decay_ref.shape[0]
    reach = taps_ref.shape[1] - 1
    run = length // LANES
    rows = 256 if length % 256 == 0 else length

    def widen(k, _):
        at = pl.ds(pl.multiple_of(k * rows, rows), rows)
        for s in range(3):
            xs[s, at, :] = x_ref[s, at, :].astype(jnp.float32)
        return 0

    lax.fori_loop(0, length // rows, widen, 0)

    def wide(row):
        return jnp.broadcast_to(row, (LANES, chans))

    first = lax.broadcasted_iota(jnp.int32, (LANES, chans), 0) == 0
    rates = [decay_ref[n : n + 1, :] for n in range(modes)]
    a = [wide(jnp.exp(-r)) for r in rates]
    taps = [[wide(taps_ref[s, j : j + 1, :]) for j in range(reach + 1)] for s in range(3)]
    zero = jnp.zeros((LANES, chans), jnp.float32)

    def column(ref, t):
        return ref[pl.ds(t, LANES, stride=run), :]

    before = []
    for s in range(3):
        for j in range(1, reach + 1):
            last = column(xs.at[s], run - j)
            before.append(jnp.where(first, 0.0, pltpu.roll(last, 1, 0)))

    def sweep(t, carry):
        past, states = carry
        feats, now = [], []
        for s in range(3):
            x = column(xs.at[s], t)
            mine = past[s * reach : (s + 1) * reach]
            f = taps[s][0] * x
            for j in range(reach):
                f = f + taps[s][j + 1] * mine[j]
            feats.append(f)
            now += [x] + list(mine[: reach - 1])
        p = (feats[1] * feats[2]).astype(jnp.bfloat16).astype(jnp.float32)
        qs[pl.ds(t, LANES, stride=run), :] = feats[0]
        ps[pl.ds(t, LANES, stride=run), :] = p
        return tuple(now), tuple(a[n] * states[n] + p for n in range(modes))

    _, ends = lax.fori_loop(0, run, sweep, (tuple(before), (zero,) * modes), unroll=2)

    starts = []
    for n in range(modes):
        through = wide(jnp.exp(-rates[n] * float(run)))
        state = zero
        for _ in range(LANES - 1):
            state = jnp.where(first, 0.0, pltpu.roll(through * state + ends[n], 1, 0))
        starts.append(state)

    gain = [wide(gain_ref[n : n + 1, :]) for n in range(modes)]
    skip = wide(skip_ref[...])

    def emit(t, states):
        p = column(ps, t)
        states = tuple(a[n] * states[n] + p for n in range(modes))
        terms = [gain[n] * states[n] for n in range(modes)] + [skip * p]
        while len(terms) > 1:
            terms = [sum(terms[k : k + 2][1:], terms[k]) for k in range(0, len(terms), 2)]
        at = pl.ds(t, LANES, stride=run)
        qs[at, :] = qs[at, :] * terms[0]
        return states

    lax.fori_loop(0, run, emit, tuple(starts), unroll=2)

    def narrow(k, _):
        at = pl.ds(pl.multiple_of(k * rows, rows), rows)
        out_ref[at, :] = qs[at, :].astype(jnp.bfloat16)
        return 0

    lax.fori_loop(0, length // rows, narrow, 0)


def convolve(projected, taps, decay, gain, skip):
    _, length, chans = projected.shape
    return pl.pallas_call(
        conv_kernel,
        out_shape=jax.ShapeDtypeStruct((length, chans), jnp.bfloat16),
        in_specs=[pl.BlockSpec(memory_space=pltpu.VMEM)] * 5,
        out_specs=pl.BlockSpec(memory_space=pltpu.VMEM),
        scratch_shapes=[
            pltpu.VMEM((3, length, chans), jnp.float32),
            pltpu.VMEM((length, chans), jnp.float32),
            pltpu.VMEM((length, chans), jnp.float32),
        ],
        compiler_params=pltpu.CompilerParams(vmem_limit_bytes=60 << 20),
    )(projected, taps, decay, gain, skip)


MESH = pl.DeviceIdType.MESH


def remote(src, dst, send, recv, device):
    return pltpu.make_async_remote_copy(
        src_ref=src, dst_ref=dst, send_sem=send, recv_sem=recv, device_id=device, device_id_type=MESH
    )


def project_kernel(
    n_ctx, cuts, tok_ref, w_hbm, out_ref, held, w, part, near, sums, far,
    w_sem, tok_sem, up_s, down_s, line_r, pair_s, pair_r, near_s, near_r, far_s, far_r,
):
    rows = held.shape[1]
    streams, _, width = w.shape
    chans = width // 4
    line = n_ctx // 2
    ctx, ch = lax.axis_index("ctx"), lax.axis_index("ch")
    z, x = lax.div(ctx, 2), lax.rem(ctx, 2)
    y, core = lax.div(ch, 2), lax.rem(ch, 2)
    near_ch, far_ch = y * 2 + 1 - core, (1 - y) * 2 + core
    has_up, has_down = z + 1 < line, z > 0

    load = pltpu.make_async_copy(w_hbm, w, w_sem)
    load.start()
    own = []
    for q in range(cuts):
        fetch = pltpu.make_async_copy(
            tok_ref.at[pl.ds(q * rows, rows), :], held.at[ctx * cuts + q], tok_sem.at[q]
        )
        fetch.start()
        own.append(fetch)

    barrier = pltpu.get_barrier_semaphore()

    def greet(*device):
        pl.semaphore_signal(barrier, inc=1, device_id=device, device_id_type=MESH)

    greet(z * 2 + 1 - x, ch)
    greet(ctx, near_ch)
    greet(ctx, far_ch)

    @pl.when(has_up)
    def _():
        greet(ctx + 2, ch)

    @pl.when(has_down)
    def _():
        greet(ctx - 2, ch)

    pl.semaphore_wait(barrier, 3 + has_up.astype(jnp.int32) + has_down.astype(jnp.int32))

    def slot(src, side):
        return (lax.div(src, cuts) * 2 + side) * cuts + lax.rem(src, cuts)

    def up_copy(src):
        at = held.at[slot(src, x)]
        return remote(at, at, up_s.at[src], line_r.at[src], (ctx + 2, ch))

    def down_copy(src):
        at = held.at[slot(src, x)]
        return remote(at, at, down_s.at[src], line_r.at[src], (ctx - 2, ch))

    def pair_copy(src, side):
        at = held.at[slot(src, side)]
        return remote(at, at, pair_s.at[src], pair_r.at[src], (z * 2 + 1 - x, ch))

    def near_copy(r):
        return remote(part.at[1 - core, r], near.at[r], near_s.at[r], near_r.at[r], (ctx, near_ch))

    def far_copy(r):
        return remote(sums.at[r], far.at[r], far_s.at[r], far_r.at[r], (ctx, far_ch))

    for q in range(cuts):
        own[q].wait()

        @pl.when(has_up)
        def _():
            up_copy(z * cuts + q).start()

        @pl.when(has_down)
        def _():
            down_copy(z * cuts + q).start()

        pair_copy(z * cuts + q, x).start()

    load.wait()

    def compute(r):
        def stream(s, _):
            for half in range(2):
                acc = jnp.dot(
                    held[r],
                    w[s, :, half * 2 * chans : (half + 1) * 2 * chans],
                    preferred_element_type=jnp.float32,
                ).astype(jnp.bfloat16)
                part[0, r, half, s] = acc[:, :chans]
                part[1, r, half, s] = acc[:, chans:]
            return 0

        lax.fori_loop(0, streams, stream, 0)
        near_copy(r).start()

    def combine(r):
        near_copy(r).wait_recv()
        for s in range(streams):
            both = part[core, r, 1 - y, s].astype(jnp.float32) + near[r, 1 - y, s].astype(jnp.float32)
            sums[r, s] = both.astype(jnp.bfloat16)
        far_copy(r).start()

    def place(t):
        s = lax.div(t + cuts, cuts) - 1
        away = lax.div(s + 1, 2)
        sign = 2 * lax.rem(s + 1, 2) - 1
        at = z + away * sign
        return at * cuts + lax.rem(t + cuts, cuts), sign, (t >= 0) & (at >= 0) & (at < line)

    def step(s, _):
        at, sign, valid = place(s)

        @pl.when(valid)
        def _():
            @pl.when(s >= cuts)
            def _():
                up_copy(at).wait_recv()

                @pl.when((sign < 0) & has_up)
                def _():
                    up_copy(at).start()

                @pl.when((sign > 0) & has_down)
                def _():
                    down_copy(at).start()

                pair_copy(at, x).start()

            compute(slot(at, x))

        at1, _, valid1 = place(s - 1)

        @pl.when(valid1)
        def _():
            pair_copy(at1, 1 - x).wait_recv()
            compute(slot(at1, 1 - x))
            combine(slot(at1, x))

        at2, _, valid2 = place(s - 2)

        @pl.when(valid2)
        def _():
            combine(slot(at2, 1 - x))

        return 0

    lax.fori_loop(0, (2 * line - 1) * cuts + 2, step, 0)

    def finish(r, _):
        far_copy(r).wait_recv()
        at = pl.ds(pl.multiple_of(r * rows, rows), rows)
        for s in range(streams):
            total = part[core, r, y, s].astype(jnp.float32) + near[r, y, s].astype(jnp.float32)
            out_ref[s, at, :] = (total + far[r, s].astype(jnp.float32)).astype(jnp.bfloat16)
        return 0

    lax.fori_loop(0, n_ctx * cuts, finish, 0)

    def drain(r, _):
        near_copy(r).wait_send()
        far_copy(r).wait_send()
        return 0

    lax.fori_loop(0, n_ctx * cuts, drain, 0)

    def drain_line(src, _):
        pair_copy(src, x).wait_send()

        @pl.when(has_up & (lax.div(src, cuts) <= z))
        def _():
            up_copy(src).wait_send()

        @pl.when(has_down & (lax.div(src, cuts) >= z))
        def _():
            down_copy(src).wait_send()

        return 0

    lax.fori_loop(0, line * cuts, drain_line, 0)


def project(tokens, in_weight):
    n_ctx = lax.axis_size("ctx")
    cuts = 2
    rows, depth = tokens.shape[0] // cuts, tokens.shape[1]
    slots = n_ctx * cuts
    streams, width = in_weight.shape[1:]
    chans = width // 4
    dma = pltpu.SemaphoreType.DMA
    line = n_ctx // 2
    return pl.pallas_call(
        functools.partial(project_kernel, n_ctx, cuts),
        out_shape=jax.ShapeDtypeStruct((streams, slots * rows, chans), jnp.bfloat16),
        in_specs=[pl.BlockSpec(memory_space=pl.ANY)] * 2,
        out_specs=pl.BlockSpec(memory_space=pltpu.VMEM),
        scratch_shapes=[
            pltpu.VMEM((slots, rows, depth), jnp.bfloat16),
            pltpu.VMEM((streams, depth, width), jnp.bfloat16),
            pltpu.VMEM((2, slots, 2, streams, rows, chans), jnp.bfloat16),
            pltpu.VMEM((slots, 2, streams, rows, chans), jnp.bfloat16),
            pltpu.VMEM((slots, streams, rows, chans), jnp.bfloat16),
            pltpu.VMEM((slots, streams, rows, chans), jnp.bfloat16),
            dma,
            dma((cuts,)),
        ]
        + [dma((line * cuts,))] * 5
        + [dma((slots,))] * 4,
        compiler_params=pltpu.CompilerParams(
            collective_id=0, has_side_effects=True, vmem_limit_bytes=62 << 20
        ),
    )(tokens, jnp.transpose(in_weight, (1, 0, 2)))


def mix_kernel(
    n_ctx, g_ref, w_hbm, out_ref, blocks, w, acc,
    w_sem, sent_s, sent_r, far_s, far_r, near_s, near_r, relay_s, relay_r,
):
    chans = g_ref.shape[2]
    width = 4 * chans
    ctx, ch = lax.axis_index("ctx"), lax.axis_index("ch")
    y, core = lax.div(ch, 2), lax.rem(ch, 2)
    near_ch, far_ch, cross_ch = y * 2 + 1 - core, (1 - y) * 2 + core, (1 - y) * 2 + 1 - core
    load = pltpu.make_async_copy(w_hbm, w, w_sem)
    load.start()

    def lanes(j):
        return pl.ds(pl.multiple_of(j * chans, chans), chans)

    def peer(k):
        return lax.rem(ctx + k, n_ctx)

    barrier = pltpu.get_barrier_semaphore()

    def greet(device):
        pl.semaphore_signal(barrier, inc=1, device_id=device, device_id_type=MESH)

    def greet_peer(k, _):
        greet((peer(k), ch))
        return 0

    lax.fori_loop(1, n_ctx, greet_peer, 0)
    greet((ctx, near_ch))
    greet((ctx, far_ch))
    blocks[ctx, :, lanes(ch)] = g_ref[ctx]
    acc[...] = jnp.zeros_like(acc)
    pl.semaphore_wait(barrier, n_ctx + 1)

    def sent_copy(dest):
        return remote(
            g_ref.at[dest], blocks.at[ctx, :, lanes(ch)], sent_s.at[dest], sent_r.at[ctx], (dest, ch)
        )

    def arrival(src):
        at = blocks.at[src, :, lanes(ch)]
        return remote(at, at, sent_s.at[src], sent_r.at[src], (src, ch))

    def far_copy(src, j):
        at = blocks.at[src, :, lanes(j)]
        return remote(at, at, far_s.at[src], far_r.at[src], (ctx, far_ch))

    def near_copy(src, j):
        at = blocks.at[src, :, lanes(j)]
        return remote(at, at, near_s.at[src], near_r.at[src], (ctx, near_ch))

    def relay_copy(src, j):
        at = blocks.at[src, :, lanes(j)]
        return remote(at, at, relay_s.at[src], relay_r.at[src], (ctx, near_ch))

    def send(k, _):
        sent_copy(peer(k)).start()
        return 0

    lax.fori_loop(1, n_ctx, send, 0)

    def step(k, _):
        @pl.when(k < n_ctx)
        def _():
            src = peer(n_ctx - k)

            @pl.when(k > 0)
            def _():
                arrival(src).wait_recv()

            far_copy(src, ch).start()
            near_copy(src, ch).start()

        @pl.when((k >= 1) & (k <= n_ctx))
        def _():
            src = peer(n_ctx - k + 1)
            far_copy(src, far_ch).wait_recv()
            relay_copy(src, far_ch).start()

        @pl.when(k == 1)
        def _():
            load.wait()

        @pl.when(k >= 2)
        def _():
            src = peer(n_ctx - k + 2)
            near_copy(src, near_ch).wait_recv()
            relay_copy(src, cross_ch).wait_recv()
            at = pl.ds(pl.multiple_of(src * width, width), width)
            acc[...] += jnp.dot(blocks[src], w[at, :], preferred_element_type=jnp.float32)

        return 0

    lax.fori_loop(0, n_ctx + 2, step, 0)
    out_ref[...] = acc[...].astype(jnp.bfloat16)

    def drain(k, _):
        src = peer(k)

        @pl.when(k > 0)
        def _():
            sent_copy(src).wait_send()

        far_copy(src, ch).wait_send()
        near_copy(src, ch).wait_send()
        relay_copy(src, far_ch).wait_send()
        return 0

    lax.fori_loop(0, n_ctx, drain, 0)


def mix(gated, out_weight):
    n_ctx, rows, chans = gated.shape
    dma = pltpu.SemaphoreType.DMA
    return pl.pallas_call(
        functools.partial(mix_kernel, n_ctx),
        out_shape=jax.ShapeDtypeStruct((rows, out_weight.shape[1]), jnp.bfloat16),
        in_specs=[pl.BlockSpec(memory_space=pltpu.VMEM), pl.BlockSpec(memory_space=pl.ANY)],
        out_specs=pl.BlockSpec(memory_space=pltpu.VMEM),
        scratch_shapes=[
            pltpu.VMEM((n_ctx, rows, 4 * chans), jnp.bfloat16),
            pltpu.VMEM(out_weight.shape, jnp.bfloat16),
            pltpu.VMEM((rows, out_weight.shape[1]), jnp.float32),
            dma,
        ]
        + [dma((n_ctx,))] * 8,
        compiler_params=pltpu.CompilerParams(
            collective_id=1, has_side_effects=True, vmem_limit_bytes=62 << 20
        ),
    )(gated, out_weight)


def own_parameters(short_filter, decay_rates, residues, skip_gain, chans):
    n_ctx, n_ch = lax.axis_size("ctx"), lax.axis_size("ch")
    start = lax.axis_index("ctx") * chans
    flat = short_filter.reshape(short_filter.shape[0], -1)
    packed = jnp.concatenate([flat, decay_rates, residues, skip_gain[:, None]], axis=1)
    piece = lax.dynamic_slice_in_dim(packed, start, chans, 0)
    pairs = []
    for s in range(n_ctx):
        for c in range(n_ch):
            pairs.append((s * n_ch + c, c * n_ctx + s))
    mine = lax.ppermute(piece, ("ctx", "ch"), pairs).T
    n_taps, order = flat.shape[1], decay_rates.shape[1]
    taps = mine[:n_taps].reshape(short_filter.shape[1], short_filter.shape[2], chans)
    decay = mine[n_taps : n_taps + order]
    gain = mine[n_taps + order : n_taps + 2 * order] * jnp.sqrt(-jnp.expm1(-2.0 * decay))
    return taps, decay, gain, mine[n_taps + 2 * order :]


def local(tokens, in_weight, short_filter, decay_rates, residues, skip_gain, out_weight):
    n_ctx, n_ch = lax.axis_size("ctx"), lax.axis_size("ch")
    rows_here = tokens.shape[0]
    chans = in_weight.shape[2] // n_ch
    taps, decay, gain, skip = own_parameters(short_filter, decay_rates, residues, skip_gain, chans)
    if n_ch == 4 and n_ctx % 2 == 0 and chans % 128 == 0:
        gated = convolve(project(tokens, in_weight), taps, decay, gain, skip)
        return mix(gated.reshape(n_ctx, rows_here, chans), out_weight)
    everyone = lax.all_gather(tokens, "ctx", axis=0, tiled=True)
    terms = jnp.einsum("rd,dsc->src", everyone, in_weight, preferred_element_type=jnp.float32)
    projected = lax.psum_scatter(terms.astype(jnp.bfloat16), "ch", scatter_dimension=2, tiled=True)
    gated = convolve(projected, taps, decay, gain, skip)
    sent = gated.reshape(n_ctx, rows_here, chans)
    mine = lax.all_to_all(sent, "ctx", split_axis=0, concat_axis=0, tiled=True)
    every = lax.all_gather(mine, "ch", axis=0)
    weight = out_weight.reshape(n_ctx, n_ch, chans, out_weight.shape[1])
    mixed = jnp.einsum("jirc,ijcd->rd", every, weight, preferred_element_type=jnp.float32)
    return mixed.astype(jnp.bfloat16)


def solution(mesh):
    in_specs = (
        P("ctx", "ch"),
        P("ch", None, "ctx"),
        P("ch", None, None),
        P("ch", None),
        P("ch", None),
        P("ch"),
        P(None, "ch"),
    )
    out_specs = P("ctx", "ch")
    return jax.shard_map(local, mesh=mesh, in_specs=in_specs, out_specs=out_specs, check_vma=False)
```

```python
import functools

import jax
import jax.numpy as jnp
from jax import lax
from jax.experimental import pallas as pl
from jax.experimental.pallas import tpu as pltpu
from jax.sharding import PartitionSpec as P

LANES = 8


def conv_kernel(x_ref, taps_ref, decay_ref, gain_ref, skip_ref, out_ref, xs, ps, qs):
    _, length, chans = x_ref.shape
    modes = decay_ref.shape[0]
    reach = taps_ref.shape[1] - 1
    run = length // LANES
    rows = 256 if length % 256 == 0 else length

    def widen(k, _):
        at = pl.ds(pl.multiple_of(k * rows, rows), rows)
        for s in range(3):
            xs[s, at, :] = x_ref[s, at, :].astype(jnp.float32)
        return 0

    lax.fori_loop(0, length // rows, widen, 0)

    def wide(row):
        return jnp.broadcast_to(row, (LANES, chans))

    first = lax.broadcasted_iota(jnp.int32, (LANES, chans), 0) == 0
    rates = [decay_ref[n : n + 1, :] for n in range(modes)]
    a = [wide(jnp.exp(-r)) for r in rates]
    taps = [[wide(taps_ref[s, j : j + 1, :]) for j in range(reach + 1)] for s in range(3)]
    zero = jnp.zeros((LANES, chans), jnp.float32)

    def column(ref, t):
        return ref[pl.ds(t, LANES, stride=run), :]

    before = []
    for s in range(3):
        for j in range(1, reach + 1):
            last = column(xs.at[s], run - j)
            before.append(jnp.where(first, 0.0, pltpu.roll(last, 1, 0)))

    def sweep(t, carry):
        past, states = carry
        feats, now = [], []
        for s in range(3):
            x = column(xs.at[s], t)
            mine = past[s * reach : (s + 1) * reach]
            f = taps[s][0] * x
            for j in range(reach):
                f = f + taps[s][j + 1] * mine[j]
            feats.append(f)
            now += [x] + list(mine[: reach - 1])
        p = (feats[1] * feats[2]).astype(jnp.bfloat16).astype(jnp.float32)
        qs[pl.ds(t, LANES, stride=run), :] = feats[0]
        ps[pl.ds(t, LANES, stride=run), :] = p
        return tuple(now), tuple(a[n] * states[n] + p for n in range(modes))

    _, ends = lax.fori_loop(0, run, sweep, (tuple(before), (zero,) * modes), unroll=2)

    starts = []
    for n in range(modes):
        through = wide(jnp.exp(-rates[n] * float(run)))
        state = zero
        for _ in range(LANES - 1):
            state = jnp.where(first, 0.0, pltpu.roll(through * state + ends[n], 1, 0))
        starts.append(state)

    gain = [wide(gain_ref[n : n + 1, :]) for n in range(modes)]
    skip = wide(skip_ref[...])

    def emit(t, states):
        p = column(ps, t)
        states = tuple(a[n] * states[n] + p for n in range(modes))
        terms = [gain[n] * states[n] for n in range(modes)] + [skip * p]
        while len(terms) > 1:
            terms = [sum(terms[k : k + 2][1:], terms[k]) for k in range(0, len(terms), 2)]
        at = pl.ds(t, LANES, stride=run)
        qs[at, :] = qs[at, :] * terms[0]
        return states

    lax.fori_loop(0, run, emit, tuple(starts), unroll=2)

    def narrow(k, _):
        at = pl.ds(pl.multiple_of(k * rows, rows), rows)
        out_ref[at, :] = qs[at, :].astype(jnp.bfloat16)
        return 0

    lax.fori_loop(0, length // rows, narrow, 0)


def convolve(projected, taps, decay, gain, skip):
    _, length, chans = projected.shape
    return pl.pallas_call(
        conv_kernel,
        out_shape=jax.ShapeDtypeStruct((length, chans), jnp.bfloat16),
        in_specs=[pl.BlockSpec(memory_space=pltpu.VMEM)] * 5,
        out_specs=pl.BlockSpec(memory_space=pltpu.VMEM),
        scratch_shapes=[
            pltpu.VMEM((3, length, chans), jnp.float32),
            pltpu.VMEM((length, chans), jnp.float32),
            pltpu.VMEM((length, chans), jnp.float32),
        ],
        compiler_params=pltpu.CompilerParams(vmem_limit_bytes=60 << 20),
    )(projected, taps, decay, gain, skip)


MESH = pl.DeviceIdType.MESH


def remote(src, dst, send, recv, device):
    return pltpu.make_async_remote_copy(
        src_ref=src, dst_ref=dst, send_sem=send, recv_sem=recv, device_id=device, device_id_type=MESH
    )


def project_kernel(
    n_ctx, cuts, tok_ref, w_hbm, out_ref, held, w, part, near, sums, far,
    w_sem, tok_sem, up_s, down_s, line_r, pair_s, pair_r, near_s, near_r, far_s, far_r,
):
    rows = held.shape[1]
    streams, _, width = w.shape
    chans = width // 4
    line = n_ctx // 2
    ctx, ch = lax.axis_index("ctx"), lax.axis_index("ch")
    z, x = lax.div(ctx, 2), lax.rem(ctx, 2)
    y, core = lax.div(ch, 2), lax.rem(ch, 2)
    near_ch, far_ch = y * 2 + 1 - core, (1 - y) * 2 + core
    has_up, has_down = z + 1 < line, z > 0

    load = pltpu.make_async_copy(w_hbm, w, w_sem)
    load.start()
    own = []
    for q in range(cuts):
        fetch = pltpu.make_async_copy(
            tok_ref.at[pl.ds(q * rows, rows), :], held.at[ctx * cuts + q], tok_sem.at[q]
        )
        fetch.start()
        own.append(fetch)

    barrier = pltpu.get_barrier_semaphore()

    def greet(*device):
        pl.semaphore_signal(barrier, inc=1, device_id=device, device_id_type=MESH)

    greet(z * 2 + 1 - x, ch)
    greet(ctx, near_ch)
    greet(ctx, far_ch)

    @pl.when(has_up)
    def _():
        greet(ctx + 2, ch)

    @pl.when(has_down)
    def _():
        greet(ctx - 2, ch)

    pl.semaphore_wait(barrier, 3 + has_up.astype(jnp.int32) + has_down.astype(jnp.int32))

    def slot(src, side):
        return (lax.div(src, cuts) * 2 + side) * cuts + lax.rem(src, cuts)

    def up_copy(src):
        at = held.at[slot(src, x)]
        return remote(at, at, up_s.at[src], line_r.at[src], (ctx + 2, ch))

    def down_copy(src):
        at = held.at[slot(src, x)]
        return remote(at, at, down_s.at[src], line_r.at[src], (ctx - 2, ch))

    def pair_copy(src, side):
        at = held.at[slot(src, side)]
        return remote(at, at, pair_s.at[src], pair_r.at[src], (z * 2 + 1 - x, ch))

    def near_copy(r):
        return remote(part.at[1 - core, r], near.at[r], near_s.at[r], near_r.at[r], (ctx, near_ch))

    def far_copy(r):
        return remote(sums.at[r], far.at[r], far_s.at[r], far_r.at[r], (ctx, far_ch))

    for q in range(cuts):
        own[q].wait()

        @pl.when(has_up)
        def _():
            up_copy(z * cuts + q).start()

        @pl.when(has_down)
        def _():
            down_copy(z * cuts + q).start()

        pair_copy(z * cuts + q, x).start()

    load.wait()

    def compute(r):
        def stream(s, _):
            for half in range(2):
                acc = jnp.dot(
                    held[r],
                    w[s, :, half * 2 * chans : (half + 1) * 2 * chans],
                    preferred_element_type=jnp.float32,
                ).astype(jnp.bfloat16)
                part[0, r, half, s] = acc[:, :chans]
                part[1, r, half, s] = acc[:, chans:]
            return 0

        lax.fori_loop(0, streams, stream, 0)
        near_copy(r).start()

    def combine(r):
        near_copy(r).wait_recv()
        for s in range(streams):
            both = part[core, r, 1 - y, s].astype(jnp.float32) + near[r, 1 - y, s].astype(jnp.float32)
            sums[r, s] = both.astype(jnp.bfloat16)
        far_copy(r).start()

    def place(t):
        s = lax.div(t + cuts, cuts) - 1
        away = lax.div(s + 1, 2)
        sign = 2 * lax.rem(s + 1, 2) - 1
        at = z + away * sign
        return at * cuts + lax.rem(t + cuts, cuts), sign, (t >= 0) & (at >= 0) & (at < line)

    def step(s, _):
        at, sign, valid = place(s)

        @pl.when(valid)
        def _():
            @pl.when(s >= cuts)
            def _():
                up_copy(at).wait_recv()

                @pl.when((sign < 0) & has_up)
                def _():
                    up_copy(at).start()

                @pl.when((sign > 0) & has_down)
                def _():
                    down_copy(at).start()

                pair_copy(at, x).start()

            compute(slot(at, x))

        at1, _, valid1 = place(s - 1)

        @pl.when(valid1)
        def _():
            pair_copy(at1, 1 - x).wait_recv()
            compute(slot(at1, 1 - x))
            combine(slot(at1, x))

        at2, _, valid2 = place(s - 2)

        @pl.when(valid2)
        def _():
            combine(slot(at2, 1 - x))

        return 0

    lax.fori_loop(0, (2 * line - 1) * cuts + 2, step, 0)

    def finish(r, _):
        far_copy(r).wait_recv()
        at = pl.ds(pl.multiple_of(r * rows, rows), rows)
        for s in range(streams):
            total = part[core, r, y, s].astype(jnp.float32) + near[r, y, s].astype(jnp.float32)
            out_ref[s, at, :] = (total + far[r, s].astype(jnp.float32)).astype(jnp.bfloat16)
        return 0

    lax.fori_loop(0, n_ctx * cuts, finish, 0)

    def drain(r, _):
        near_copy(r).wait_send()
        far_copy(r).wait_send()
        return 0

    lax.fori_loop(0, n_ctx * cuts, drain, 0)

    def drain_line(src, _):
        pair_copy(src, x).wait_send()

        @pl.when(has_up & (lax.div(src, cuts) <= z))
        def _():
            up_copy(src).wait_send()

        @pl.when(has_down & (lax.div(src, cuts) >= z))
        def _():
            down_copy(src).wait_send()

        return 0

    lax.fori_loop(0, line * cuts, drain_line, 0)


def project(tokens, in_weight):
    n_ctx = lax.axis_size("ctx")
    cuts = 2
    rows, depth = tokens.shape[0] // cuts, tokens.shape[1]
    slots = n_ctx * cuts
    streams, width = in_weight.shape[1:]
    chans = width // 4
    dma = pltpu.SemaphoreType.DMA
    line = n_ctx // 2
    return pl.pallas_call(
        functools.partial(project_kernel, n_ctx, cuts),
        out_shape=jax.ShapeDtypeStruct((streams, slots * rows, chans), jnp.bfloat16),
        in_specs=[pl.BlockSpec(memory_space=pl.ANY)] * 2,
        out_specs=pl.BlockSpec(memory_space=pltpu.VMEM),
        scratch_shapes=[
            pltpu.VMEM((slots, rows, depth), jnp.bfloat16),
            pltpu.VMEM((streams, depth, width), jnp.bfloat16),
            pltpu.VMEM((2, slots, 2, streams, rows, chans), jnp.bfloat16),
            pltpu.VMEM((slots, 2, streams, rows, chans), jnp.bfloat16),
            pltpu.VMEM((slots, streams, rows, chans), jnp.bfloat16),
            pltpu.VMEM((slots, streams, rows, chans), jnp.bfloat16),
            dma,
            dma((cuts,)),
        ]
        + [dma((line * cuts,))] * 5
        + [dma((slots,))] * 4,
        compiler_params=pltpu.CompilerParams(
            collective_id=0, has_side_effects=True, vmem_limit_bytes=62 << 20
        ),
    )(tokens, jnp.transpose(in_weight, (1, 0, 2)))


def mix_kernel(
    n_ctx, x_ref, taps_ref, decay_ref, gain_ref, skip_ref, w_hbm, out_ref,
    g_ref, xs, ps, qs, entering, blocks, w, acc,
    w_sem, sent_s, sent_r, far_s, far_r, near_s, near_r, relay_s, relay_r,
):
    _, rows, chans = g_ref.shape
    modes = decay_ref.shape[0]
    reach = taps_ref.shape[1] - 1
    run = rows // LANES
    width = 4 * chans
    ctx, ch = lax.axis_index("ctx"), lax.axis_index("ch")
    y, core = lax.div(ch, 2), lax.rem(ch, 2)
    near_ch, far_ch, cross_ch = y * 2 + 1 - core, (1 - y) * 2 + core, (1 - y) * 2 + 1 - core
    load = pltpu.make_async_copy(w_hbm, w, w_sem)
    load.start()

    def lanes(j):
        return pl.ds(pl.multiple_of(j * chans, chans), chans)

    def peer(k):
        return lax.rem(ctx + k, n_ctx)

    barrier = pltpu.get_barrier_semaphore()

    def greet(device):
        pl.semaphore_signal(barrier, inc=1, device_id=device, device_id_type=MESH)

    def greet_peer(k, _):
        greet((peer(k), ch))
        return 0

    lax.fori_loop(1, n_ctx, greet_peer, 0)
    greet((ctx, near_ch))
    greet((ctx, far_ch))
    acc[...] = jnp.zeros_like(acc)

    def wide(row):
        return jnp.broadcast_to(row, (LANES, chans))

    sub = lax.broadcasted_iota(jnp.int32, (LANES, chans), 0)
    zero = jnp.zeros((LANES, chans), jnp.float32)
    rates = [decay_ref[n : n + 1, :] for n in range(modes)]
    a = [wide(jnp.exp(-r)) for r in rates]
    taps = [[wide(taps_ref[s, j : j + 1, :]) for j in range(reach + 1)] for s in range(3)]
    for s in range(3):
        xs[s, 0:8, :] = jnp.zeros((8, chans), jnp.float32)

    def absorb(k, carry):
        base = pl.multiple_of(k * rows, rows)
        for s in range(3):
            xs[s, pl.ds(base + 8, rows), :] = x_ref[s, pl.ds(base, rows), :].astype(jnp.float32)
        before = []
        for s in range(3):
            for j in range(1, reach + 1):
                before.append(xs[s, pl.ds(base + 8 - j, LANES, stride=run), :])

        def sweep(t, inner):
            past, states = inner
            feats, now = [], []
            for s in range(3):
                x = xs[s, pl.ds(base + 8 + t, LANES, stride=run), :]
                mine = past[s * reach : (s + 1) * reach]
                f = taps[s][0] * x
                for j in range(reach):
                    f = f + taps[s][j + 1] * mine[j]
                feats.append(f)
                now += [x] + list(mine[: reach - 1])
            p = (feats[1] * feats[2]).astype(jnp.bfloat16).astype(jnp.float32)
            qs[pl.ds(base + t, LANES, stride=run), :] = feats[0]
            ps[pl.ds(base + t, LANES, stride=run), :] = p
            return tuple(now), tuple(a[n] * states[n] + p for n in range(modes))

        _, ends = lax.fori_loop(0, run, sweep, (tuple(before), (zero,) * modes), unroll=2)
        following = []
        for n in range(modes):
            through = wide(jnp.exp(-rates[n] * float(run)))
            state = jnp.where(sub == 0, carry[n], pltpu.roll(ends[n], 1, 0))
            power, by = through, 1
            while by < LANES:
                state = state + jnp.where(sub >= by, power * pltpu.roll(state, by, 0), 0.0)
                power, by = power * power, by * 2
            entering[k, n] = state
            following.append(pltpu.roll(through * state + ends[n], 1, 0))
        return tuple(following)

    lax.fori_loop(0, n_ctx, absorb, (zero,) * modes)
    pl.semaphore_wait(barrier, n_ctx + 1)
    gain = [wide(gain_ref[n : n + 1, :]) for n in range(modes)]
    skip = wide(skip_ref[...])

    def emit_block(k):
        base = pl.multiple_of(k * rows, rows)

        def emit(t, states):
            at = pl.ds(base + t, LANES, stride=run)
            p = ps[at, :]
            states = tuple(a[n] * states[n] + p for n in range(modes))
            terms = [gain[n] * states[n] for n in range(modes)] + [skip * p]
            while len(terms) > 1:
                terms = [sum(terms[i : i + 2][1:], terms[i]) for i in range(0, len(terms), 2)]
            qs[at, :] = qs[at, :] * terms[0]
            return states

        lax.fori_loop(0, run, emit, tuple(entering[k, n] for n in range(modes)), unroll=2)
        g_ref[k] = qs[pl.ds(base, rows), :].astype(jnp.bfloat16)

    def offset(k):
        odd = lax.rem(k, 2)
        return n_ctx // 2 + (1 - odd) * lax.div(k, 2) - odd * lax.div(k + 1, 2)

    def sent_copy(dest):
        return remote(
            g_ref.at[dest], blocks.at[ctx, :, lanes(ch)], sent_s.at[dest], sent_r.at[ctx], (dest, ch)
        )

    def arrival(src):
        at = blocks.at[src, :, lanes(ch)]
        return remote(at, at, sent_s.at[src], sent_r.at[src], (src, ch))

    def far_copy(src, j):
        at = blocks.at[src, :, lanes(j)]
        return remote(at, at, far_s.at[src], far_r.at[src], (ctx, far_ch))

    def near_copy(src, j):
        at = blocks.at[src, :, lanes(j)]
        return remote(at, at, near_s.at[src], near_r.at[src], (ctx, near_ch))

    def relay_copy(src, j):
        at = blocks.at[src, :, lanes(j)]
        return remote(at, at, relay_s.at[src], relay_r.at[src], (ctx, near_ch))

    def send(k, _):
        dest = peer(offset(k))
        emit_block(dest)

        @pl.when(k < n_ctx - 1)
        def _():
            sent_copy(dest).start()

        return 0

    lax.fori_loop(0, n_ctx, send, 0)
    blocks[ctx, :, lanes(ch)] = g_ref[ctx]

    def source(k):
        own = jnp.where(k == 0, 0, n_ctx - offset(k - 1))
        return lax.rem(ctx + own, n_ctx)

    def step(k, _):
        @pl.when(k < n_ctx)
        def _():
            src = source(k)

            @pl.when(k > 0)
            def _():
                arrival(src).wait_recv()

            far_copy(src, ch).start()
            near_copy(src, ch).start()

        @pl.when((k >= 1) & (k <= n_ctx))
        def _():
            src = source(k - 1)
            far_copy(src, far_ch).wait_recv()
            relay_copy(src, far_ch).start()

        @pl.when(k == 1)
        def _():
            load.wait()

        @pl.when(k >= 2)
        def _():
            src = source(k - 2)
            near_copy(src, near_ch).wait_recv()
            relay_copy(src, cross_ch).wait_recv()
            at = pl.ds(pl.multiple_of(src * width, width), width)
            acc[...] += jnp.dot(blocks[src], w[at, :], preferred_element_type=jnp.float32)

        return 0

    lax.fori_loop(0, n_ctx + 2, step, 0)
    out_ref[...] = acc[...].astype(jnp.bfloat16)

    def drain(k, _):
        src = peer(k)

        @pl.when(k > 0)
        def _():
            sent_copy(src).wait_send()

        far_copy(src, ch).wait_send()
        near_copy(src, ch).wait_send()
        relay_copy(src, far_ch).wait_send()
        return 0

    lax.fori_loop(0, n_ctx, drain, 0)


def mix(projected, taps, decay, gain, skip, out_weight):
    n_ctx = lax.axis_size("ctx")
    streams, length, chans = projected.shape
    rows = length // n_ctx
    dma = pltpu.SemaphoreType.DMA
    return pl.pallas_call(
        functools.partial(mix_kernel, n_ctx),
        out_shape=jax.ShapeDtypeStruct((rows, out_weight.shape[1]), jnp.bfloat16),
        in_specs=[pl.BlockSpec(memory_space=pltpu.VMEM)] * 5 + [pl.BlockSpec(memory_space=pl.ANY)],
        out_specs=pl.BlockSpec(memory_space=pltpu.VMEM),
        scratch_shapes=[
            pltpu.VMEM((n_ctx, rows, chans), jnp.bfloat16),
            pltpu.VMEM((streams, length + 8, chans), jnp.float32),
            pltpu.VMEM((length, chans), jnp.float32),
            pltpu.VMEM((length, chans), jnp.float32),
            pltpu.VMEM((n_ctx, decay.shape[0], LANES, chans), jnp.float32),
            pltpu.VMEM((n_ctx, rows, 4 * chans), jnp.bfloat16),
            pltpu.VMEM(out_weight.shape, jnp.bfloat16),
            pltpu.VMEM((rows, out_weight.shape[1]), jnp.float32),
            dma,
        ]
        + [dma((n_ctx,))] * 8,
        compiler_params=pltpu.CompilerParams(
            collective_id=1, has_side_effects=True, vmem_limit_bytes=62 << 20
        ),
    )(projected, taps, decay, gain, skip, out_weight)


def own_parameters(short_filter, decay_rates, residues, skip_gain, chans):
    n_ctx, n_ch = lax.axis_size("ctx"), lax.axis_size("ch")
    start = lax.axis_index("ctx") * chans
    flat = short_filter.reshape(short_filter.shape[0], -1)
    packed = jnp.concatenate([flat, decay_rates, residues, skip_gain[:, None]], axis=1)
    piece = lax.dynamic_slice_in_dim(packed, start, chans, 0)
    pairs = []
    for s in range(n_ctx):
        for c in range(n_ch):
            pairs.append((s * n_ch + c, c * n_ctx + s))
    mine = lax.ppermute(piece, ("ctx", "ch"), pairs).T
    n_taps, order = flat.shape[1], decay_rates.shape[1]
    taps = mine[:n_taps].reshape(short_filter.shape[1], short_filter.shape[2], chans)
    decay = mine[n_taps : n_taps + order]
    gain = mine[n_taps + order : n_taps + 2 * order] * jnp.sqrt(-jnp.expm1(-2.0 * decay))
    return taps, decay, gain, mine[n_taps + 2 * order :]


def local(tokens, in_weight, short_filter, decay_rates, residues, skip_gain, out_weight):
    n_ctx, n_ch = lax.axis_size("ctx"), lax.axis_size("ch")
    rows_here = tokens.shape[0]
    chans = in_weight.shape[2] // n_ch
    taps, decay, gain, skip = own_parameters(short_filter, decay_rates, residues, skip_gain, chans)
    if n_ch == 4 and n_ctx % 2 == 0 and chans % 128 == 0 and rows_here % 64 == 0:
        return mix(project(tokens, in_weight), taps, decay, gain, skip, out_weight)
    everyone = lax.all_gather(tokens, "ctx", axis=0, tiled=True)
    terms = jnp.einsum("rd,dsc->src", everyone, in_weight, preferred_element_type=jnp.float32)
    projected = lax.psum_scatter(terms.astype(jnp.bfloat16), "ch", scatter_dimension=2, tiled=True)
    gated = convolve(projected, taps, decay, gain, skip)
    sent = gated.reshape(n_ctx, rows_here, chans)
    mine = lax.all_to_all(sent, "ctx", split_axis=0, concat_axis=0, tiled=True)
    every = lax.all_gather(mine, "ch", axis=0)
    weight = out_weight.reshape(n_ctx, n_ch, chans, out_weight.shape[1])
    mixed = jnp.einsum("jirc,ijcd->rd", every, weight, preferred_element_type=jnp.float32)
    return mixed.astype(jnp.bfloat16)


def solution(mesh):
    in_specs = (
        P("ctx", "ch"),
        P("ch", None, "ctx"),
        P("ch", None, None),
        P("ch", None),
        P("ch", None),
        P("ch"),
        P(None, "ch"),
    )
    out_specs = P("ctx", "ch")
    return jax.shard_map(local, mesh=mesh, in_specs=in_specs, out_specs=out_specs, check_vma=False)
```

```python
import functools

import jax
import jax.numpy as jnp
from jax import lax
from jax.experimental import pallas as pl
from jax.experimental.pallas import tpu as pltpu
from jax.sharding import PartitionSpec as P

LANES = 8


def conv_kernel(x_ref, taps_ref, decay_ref, gain_ref, skip_ref, out_ref, xs, ps, qs):
    _, length, chans = x_ref.shape
    modes = decay_ref.shape[0]
    reach = taps_ref.shape[1] - 1
    run = length // LANES
    rows = 256 if length % 256 == 0 else length

    def widen(k, _):
        at = pl.ds(pl.multiple_of(k * rows, rows), rows)
        for s in range(3):
            xs[s, at, :] = x_ref[s, at, :].astype(jnp.float32)
        return 0

    lax.fori_loop(0, length // rows, widen, 0)

    def wide(row):
        return jnp.broadcast_to(row, (LANES, chans))

    first = lax.broadcasted_iota(jnp.int32, (LANES, chans), 0) == 0
    rates = [decay_ref[n : n + 1, :] for n in range(modes)]
    a = [wide(jnp.exp(-r)) for r in rates]
    taps = [[wide(taps_ref[s, j : j + 1, :]) for j in range(reach + 1)] for s in range(3)]
    zero = jnp.zeros((LANES, chans), jnp.float32)

    def column(ref, t):
        return ref[pl.ds(t, LANES, stride=run), :]

    before = []
    for s in range(3):
        for j in range(1, reach + 1):
            last = column(xs.at[s], run - j)
            before.append(jnp.where(first, 0.0, pltpu.roll(last, 1, 0)))

    def sweep(t, carry):
        past, states = carry
        feats, now = [], []
        for s in range(3):
            x = column(xs.at[s], t)
            mine = past[s * reach : (s + 1) * reach]
            f = taps[s][0] * x
            for j in range(reach):
                f = f + taps[s][j + 1] * mine[j]
            feats.append(f)
            now += [x] + list(mine[: reach - 1])
        p = (feats[1] * feats[2]).astype(jnp.bfloat16).astype(jnp.float32)
        qs[pl.ds(t, LANES, stride=run), :] = feats[0]
        ps[pl.ds(t, LANES, stride=run), :] = p
        return tuple(now), tuple(a[n] * states[n] + p for n in range(modes))

    _, ends = lax.fori_loop(0, run, sweep, (tuple(before), (zero,) * modes), unroll=2)

    starts = []
    for n in range(modes):
        through = wide(jnp.exp(-rates[n] * float(run)))
        state = zero
        for _ in range(LANES - 1):
            state = jnp.where(first, 0.0, pltpu.roll(through * state + ends[n], 1, 0))
        starts.append(state)

    gain = [wide(gain_ref[n : n + 1, :]) for n in range(modes)]
    skip = wide(skip_ref[...])

    def emit(t, states):
        p = column(ps, t)
        states = tuple(a[n] * states[n] + p for n in range(modes))
        terms = [gain[n] * states[n] for n in range(modes)] + [skip * p]
        while len(terms) > 1:
            terms = [sum(terms[k : k + 2][1:], terms[k]) for k in range(0, len(terms), 2)]
        at = pl.ds(t, LANES, stride=run)
        qs[at, :] = qs[at, :] * terms[0]
        return states

    lax.fori_loop(0, run, emit, tuple(starts), unroll=2)

    def narrow(k, _):
        at = pl.ds(pl.multiple_of(k * rows, rows), rows)
        out_ref[at, :] = qs[at, :].astype(jnp.bfloat16)
        return 0

    lax.fori_loop(0, length // rows, narrow, 0)


def convolve(projected, taps, decay, gain, skip):
    _, length, chans = projected.shape
    return pl.pallas_call(
        conv_kernel,
        out_shape=jax.ShapeDtypeStruct((length, chans), jnp.bfloat16),
        in_specs=[pl.BlockSpec(memory_space=pltpu.VMEM)] * 5,
        out_specs=pl.BlockSpec(memory_space=pltpu.VMEM),
        scratch_shapes=[
            pltpu.VMEM((3, length, chans), jnp.float32),
            pltpu.VMEM((length, chans), jnp.float32),
            pltpu.VMEM((length, chans), jnp.float32),
        ],
        compiler_params=pltpu.CompilerParams(vmem_limit_bytes=60 << 20),
    )(projected, taps, decay, gain, skip)


MESH = pl.DeviceIdType.MESH


def remote(src, dst, send, recv, device):
    return pltpu.make_async_remote_copy(
        src_ref=src, dst_ref=dst, send_sem=send, recv_sem=recv, device_id=device, device_id_type=MESH
    )


def project_kernel(
    n_ctx, cuts, tok_ref, w_hbm, out_ref, held, w, part, near, sums, far,
    w_sem, tok_sem, up_s, down_s, line_r, pair_s, pair_r, near_s, near_r, far_s, far_r,
):
    rows = held.shape[1]
    streams, _, width = w.shape
    chans = width // 4
    line = n_ctx // 2
    ctx, ch = lax.axis_index("ctx"), lax.axis_index("ch")
    z, x = lax.div(ctx, 2), lax.rem(ctx, 2)
    y, core = lax.div(ch, 2), lax.rem(ch, 2)
    near_ch, far_ch = y * 2 + 1 - core, (1 - y) * 2 + core
    has_up, has_down = z + 1 < line, z > 0

    load = pltpu.make_async_copy(w_hbm, w, w_sem)
    load.start()
    own = []
    for q in range(cuts):
        fetch = pltpu.make_async_copy(
            tok_ref.at[pl.ds(q * rows, rows), :], held.at[ctx * cuts + q], tok_sem.at[q]
        )
        fetch.start()
        own.append(fetch)

    barrier = pltpu.get_barrier_semaphore()

    def greet(*device):
        pl.semaphore_signal(barrier, inc=1, device_id=device, device_id_type=MESH)

    greet(z * 2 + 1 - x, ch)
    greet(ctx, near_ch)
    greet(ctx, far_ch)

    @pl.when(has_up)
    def _():
        greet(ctx + 2, ch)

    @pl.when(has_down)
    def _():
        greet(ctx - 2, ch)

    pl.semaphore_wait(barrier, 3 + has_up.astype(jnp.int32) + has_down.astype(jnp.int32))

    def slot(src, side):
        return (lax.div(src, cuts) * 2 + side) * cuts + lax.rem(src, cuts)

    def up_copy(src):
        at = held.at[slot(src, x)]
        return remote(at, at, up_s.at[src], line_r.at[src], (ctx + 2, ch))

    def down_copy(src):
        at = held.at[slot(src, x)]
        return remote(at, at, down_s.at[src], line_r.at[src], (ctx - 2, ch))

    def pair_copy(src, side):
        at = held.at[slot(src, side)]
        return remote(at, at, pair_s.at[src], pair_r.at[src], (z * 2 + 1 - x, ch))

    def near_copy(r):
        return remote(part.at[1 - core, r], near.at[r], near_s.at[r], near_r.at[r], (ctx, near_ch))

    def far_copy(r):
        return remote(sums.at[r], far.at[r], far_s.at[r], far_r.at[r], (ctx, far_ch))

    for q in range(cuts):
        own[q].wait()

        @pl.when(has_up)
        def _():
            up_copy(z * cuts + q).start()

        @pl.when(has_down)
        def _():
            down_copy(z * cuts + q).start()

        pair_copy(z * cuts + q, x).start()

    load.wait()

    def compute(r):
        def stream(s, _):
            for half in range(2):
                acc = jnp.dot(
                    held[r],
                    w[s, :, half * 2 * chans : (half + 1) * 2 * chans],
                    preferred_element_type=jnp.float32,
                ).astype(jnp.bfloat16)
                part[0, r, half, s] = acc[:, :chans]
                part[1, r, half, s] = acc[:, chans:]
            return 0

        lax.fori_loop(0, streams, stream, 0)
        near_copy(r).start()

    def combine(r):
        near_copy(r).wait_recv()
        for s in range(streams):
            both = part[core, r, 1 - y, s].astype(jnp.float32) + near[r, 1 - y, s].astype(jnp.float32)
            sums[r, s] = both.astype(jnp.bfloat16)
        far_copy(r).start()

    late = 2 * cuts - 1

    def place(t):
        s = lax.div(t + cuts, cuts) - 1
        away = lax.div(s + 1, 2)
        sign = 2 * lax.rem(s + 1, 2) - 1
        at = z + away * sign
        return at * cuts + lax.rem(t + cuts, cuts), sign, (t >= 0) & (at >= 0) & (at < line)

    def step(s, _):
        at, sign, valid = place(s)

        @pl.when(valid)
        def _():
            @pl.when(s >= cuts)
            def _():
                up_copy(at).wait_recv()

                @pl.when((sign < 0) & has_up)
                def _():
                    up_copy(at).start()

                @pl.when((sign > 0) & has_down)
                def _():
                    down_copy(at).start()

                pair_copy(at, x).start()

            compute(slot(at, x))

        at1, _, valid1 = place(s - late)

        @pl.when(valid1)
        def _():
            pair_copy(at1, 1 - x).wait_recv()
            compute(slot(at1, 1 - x))

        at3, _, valid3 = place(s - 1)

        @pl.when(valid3)
        def _():
            combine(slot(at3, x))

        at2, _, valid2 = place(s - late - 1)

        @pl.when(valid2)
        def _():
            combine(slot(at2, 1 - x))

        return 0

    lax.fori_loop(0, (2 * line - 1) * cuts + late + 1, step, 0)

    def finish(r, _):
        far_copy(r).wait_recv()
        at = pl.ds(pl.multiple_of(r * rows, rows), rows)
        for s in range(streams):
            total = part[core, r, y, s].astype(jnp.float32) + near[r, y, s].astype(jnp.float32)
            out_ref[s, at, :] = (total + far[r, s].astype(jnp.float32)).astype(jnp.bfloat16)
        return 0

    lax.fori_loop(0, n_ctx * cuts, finish, 0)

    def drain(r, _):
        near_copy(r).wait_send()
        far_copy(r).wait_send()
        return 0

    lax.fori_loop(0, n_ctx * cuts, drain, 0)

    def drain_line(src, _):
        pair_copy(src, x).wait_send()

        @pl.when(has_up & (lax.div(src, cuts) <= z))
        def _():
            up_copy(src).wait_send()

        @pl.when(has_down & (lax.div(src, cuts) >= z))
        def _():
            down_copy(src).wait_send()

        return 0

    lax.fori_loop(0, line * cuts, drain_line, 0)


def project(tokens, in_weight):
    n_ctx = lax.axis_size("ctx")
    cuts = 2
    rows, depth = tokens.shape[0] // cuts, tokens.shape[1]
    slots = n_ctx * cuts
    streams, width = in_weight.shape[1:]
    chans = width // 4
    dma = pltpu.SemaphoreType.DMA
    line = n_ctx // 2
    return pl.pallas_call(
        functools.partial(project_kernel, n_ctx, cuts),
        out_shape=jax.ShapeDtypeStruct((streams, slots * rows, chans), jnp.bfloat16),
        in_specs=[pl.BlockSpec(memory_space=pl.ANY)] * 2,
        out_specs=pl.BlockSpec(memory_space=pltpu.VMEM),
        scratch_shapes=[
            pltpu.VMEM((slots, rows, depth), jnp.bfloat16),
            pltpu.VMEM((streams, depth, width), jnp.bfloat16),
            pltpu.VMEM((2, slots, 2, streams, rows, chans), jnp.bfloat16),
            pltpu.VMEM((slots, 2, streams, rows, chans), jnp.bfloat16),
            pltpu.VMEM((slots, streams, rows, chans), jnp.bfloat16),
            pltpu.VMEM((slots, streams, rows, chans), jnp.bfloat16),
            dma,
            dma((cuts,)),
        ]
        + [dma((line * cuts,))] * 5
        + [dma((slots,))] * 4,
        compiler_params=pltpu.CompilerParams(
            collective_id=0, has_side_effects=True, vmem_limit_bytes=62 << 20
        ),
    )(tokens, jnp.transpose(in_weight, (1, 0, 2)))


def mix_kernel(
    n_ctx, x_ref, taps_ref, decay_ref, gain_ref, skip_ref, w_hbm, out_ref,
    g_ref, xs, ps, qs, entering, blocks, w, acc,
    w_sem, sent_s, sent_r, far_s, far_r, near_s, near_r, relay_s, relay_r,
):
    _, rows, chans = g_ref.shape
    modes = decay_ref.shape[0]
    reach = taps_ref.shape[1] - 1
    run = rows // LANES
    width = 4 * chans
    ctx, ch = lax.axis_index("ctx"), lax.axis_index("ch")
    y, core = lax.div(ch, 2), lax.rem(ch, 2)
    near_ch, far_ch, cross_ch = y * 2 + 1 - core, (1 - y) * 2 + core, (1 - y) * 2 + 1 - core
    load = pltpu.make_async_copy(w_hbm, w, w_sem)
    load.start()

    def lanes(j):
        return pl.ds(pl.multiple_of(j * chans, chans), chans)

    def peer(k):
        return lax.rem(ctx + k, n_ctx)

    barrier = pltpu.get_barrier_semaphore()

    def greet(device):
        pl.semaphore_signal(barrier, inc=1, device_id=device, device_id_type=MESH)

    def greet_peer(k, _):
        greet((peer(k), ch))
        return 0

    lax.fori_loop(1, n_ctx, greet_peer, 0)
    greet((ctx, near_ch))
    greet((ctx, far_ch))
    acc[...] = jnp.zeros_like(acc)

    def wide(row):
        return jnp.broadcast_to(row, (LANES, chans))

    sub = lax.broadcasted_iota(jnp.int32, (LANES, chans), 0)
    zero = jnp.zeros((LANES, chans), jnp.float32)
    rates = [decay_ref[n : n + 1, :] for n in range(modes)]
    a = [wide(jnp.exp(-r)) for r in rates]
    taps = [[wide(taps_ref[s, j : j + 1, :]) for j in range(reach + 1)] for s in range(3)]
    for s in range(3):
        xs[s, 0:8, :] = jnp.zeros((8, chans), jnp.float32)

    def absorb(k, carry):
        base = pl.multiple_of(k * rows, rows)
        for s in range(3):
            xs[s, pl.ds(base + 8, rows), :] = x_ref[s, pl.ds(base, rows), :].astype(jnp.float32)
        before = []
        for s in range(3):
            for j in range(1, reach + 1):
                before.append(xs[s, pl.ds(base + 8 - j, LANES, stride=run), :])

        def sweep(t, inner):
            past, states = inner
            feats, now = [], []
            for s in range(3):
                x = xs[s, pl.ds(base + 8 + t, LANES, stride=run), :]
                mine = past[s * reach : (s + 1) * reach]
                f = taps[s][0] * x
                for j in range(reach):
                    f = f + taps[s][j + 1] * mine[j]
                feats.append(f)
                now += [x] + list(mine[: reach - 1])
            p = (feats[1] * feats[2]).astype(jnp.bfloat16).astype(jnp.float32)
            qs[pl.ds(base + t, LANES, stride=run), :] = feats[0]
            ps[pl.ds(base + t, LANES, stride=run), :] = p
            return tuple(now), tuple(a[n] * states[n] + p for n in range(modes))

        _, ends = lax.fori_loop(0, run, sweep, (tuple(before), (zero,) * modes), unroll=2)
        following = []
        for n in range(modes):
            through = wide(jnp.exp(-rates[n] * float(run)))
            state = jnp.where(sub == 0, carry[n], pltpu.roll(ends[n], 1, 0))
            power, by = through, 1
            while by < LANES:
                state = state + jnp.where(sub >= by, power * pltpu.roll(state, by, 0), 0.0)
                power, by = power * power, by * 2
            entering[k, n] = state
            following.append(pltpu.roll(through * state + ends[n], 1, 0))
        return tuple(following)

    lax.fori_loop(0, n_ctx, absorb, (zero,) * modes)
    pl.semaphore_wait(barrier, n_ctx + 1)
    gain = [wide(gain_ref[n : n + 1, :]) for n in range(modes)]
    skip = wide(skip_ref[...])

    def emit_block(k):
        base = pl.multiple_of(k * rows, rows)

        def emit(t, states):
            at = pl.ds(base + t, LANES, stride=run)
            p = ps[at, :]
            states = tuple(a[n] * states[n] + p for n in range(modes))
            terms = [gain[n] * states[n] for n in range(modes)] + [skip * p]
            while len(terms) > 1:
                terms = [sum(terms[i : i + 2][1:], terms[i]) for i in range(0, len(terms), 2)]
            qs[at, :] = qs[at, :] * terms[0]
            return states

        lax.fori_loop(0, run, emit, tuple(entering[k, n] for n in range(modes)), unroll=2)
        g_ref[k] = qs[pl.ds(base, rows), :].astype(jnp.bfloat16)

    def offset(k):
        odd = lax.rem(k, 2)
        return n_ctx // 2 + (1 - odd) * lax.div(k, 2) - odd * lax.div(k + 1, 2)

    def sent_copy(dest):
        return remote(
            g_ref.at[dest], blocks.at[ctx, :, lanes(ch)], sent_s.at[dest], sent_r.at[ctx], (dest, ch)
        )

    def arrival(src):
        at = blocks.at[src, :, lanes(ch)]
        return remote(at, at, sent_s.at[src], sent_r.at[src], (src, ch))

    def far_copy(src, j):
        at = blocks.at[src, :, lanes(j)]
        return remote(at, at, far_s.at[src], far_r.at[src], (ctx, far_ch))

    def near_copy(src, j):
        at = blocks.at[src, :, lanes(j)]
        return remote(at, at, near_s.at[src], near_r.at[src], (ctx, near_ch))

    def relay_copy(src, j):
        at = blocks.at[src, :, lanes(j)]
        return remote(at, at, relay_s.at[src], relay_r.at[src], (ctx, near_ch))

    def send(k, _):
        dest = peer(offset(k))
        emit_block(dest)

        @pl.when(k < n_ctx - 1)
        def _():
            sent_copy(dest).start()

        return 0

    lax.fori_loop(0, n_ctx, send, 0)
    blocks[ctx, :, lanes(ch)] = g_ref[ctx]

    def source(k):
        own = jnp.where(k == 0, 0, n_ctx - offset(k - 1))
        return lax.rem(ctx + own, n_ctx)

    def step(k, _):
        @pl.when(k < n_ctx)
        def _():
            src = source(k)

            @pl.when(k > 0)
            def _():
                arrival(src).wait_recv()

            far_copy(src, ch).start()
            near_copy(src, ch).start()

        @pl.when((k >= 1) & (k <= n_ctx))
        def _():
            src = source(k - 1)
            far_copy(src, far_ch).wait_recv()
            relay_copy(src, far_ch).start()

        @pl.when(k == 1)
        def _():
            load.wait()

        @pl.when(k >= 2)
        def _():
            src = source(k - 2)
            near_copy(src, near_ch).wait_recv()
            relay_copy(src, cross_ch).wait_recv()
            at = pl.ds(pl.multiple_of(src * width, width), width)
            acc[...] += jnp.dot(blocks[src], w[at, :], preferred_element_type=jnp.float32)

        return 0

    lax.fori_loop(0, n_ctx + 2, step, 0)
    out_ref[...] = acc[...].astype(jnp.bfloat16)

    def drain(k, _):
        src = peer(k)

        @pl.when(k > 0)
        def _():
            sent_copy(src).wait_send()

        far_copy(src, ch).wait_send()
        near_copy(src, ch).wait_send()
        relay_copy(src, far_ch).wait_send()
        return 0

    lax.fori_loop(0, n_ctx, drain, 0)


def mix(projected, taps, decay, gain, skip, out_weight):
    n_ctx = lax.axis_size("ctx")
    streams, length, chans = projected.shape
    rows = length // n_ctx
    dma = pltpu.SemaphoreType.DMA
    return pl.pallas_call(
        functools.partial(mix_kernel, n_ctx),
        out_shape=jax.ShapeDtypeStruct((rows, out_weight.shape[1]), jnp.bfloat16),
        in_specs=[pl.BlockSpec(memory_space=pltpu.VMEM)] * 5 + [pl.BlockSpec(memory_space=pl.ANY)],
        out_specs=pl.BlockSpec(memory_space=pltpu.VMEM),
        scratch_shapes=[
            pltpu.VMEM((n_ctx, rows, chans), jnp.bfloat16),
            pltpu.VMEM((streams, length + 8, chans), jnp.float32),
            pltpu.VMEM((length, chans), jnp.float32),
            pltpu.VMEM((length, chans), jnp.float32),
            pltpu.VMEM((n_ctx, decay.shape[0], LANES, chans), jnp.float32),
            pltpu.VMEM((n_ctx, rows, 4 * chans), jnp.bfloat16),
            pltpu.VMEM(out_weight.shape, jnp.bfloat16),
            pltpu.VMEM((rows, out_weight.shape[1]), jnp.float32),
            dma,
        ]
        + [dma((n_ctx,))] * 8,
        compiler_params=pltpu.CompilerParams(
            collective_id=1, has_side_effects=True, vmem_limit_bytes=62 << 20
        ),
    )(projected, taps, decay, gain, skip, out_weight)


def own_parameters(short_filter, decay_rates, residues, skip_gain, chans):
    n_ctx, n_ch = lax.axis_size("ctx"), lax.axis_size("ch")
    start = lax.axis_index("ctx") * chans
    flat = short_filter.reshape(short_filter.shape[0], -1)
    packed = jnp.concatenate([flat, decay_rates, residues, skip_gain[:, None]], axis=1)
    piece = lax.dynamic_slice_in_dim(packed, start, chans, 0)
    pairs = []
    for s in range(n_ctx):
        for c in range(n_ch):
            pairs.append((s * n_ch + c, c * n_ctx + s))
    mine = lax.ppermute(piece, ("ctx", "ch"), pairs).T
    n_taps, order = flat.shape[1], decay_rates.shape[1]
    taps = mine[:n_taps].reshape(short_filter.shape[1], short_filter.shape[2], chans)
    decay = mine[n_taps : n_taps + order]
    gain = mine[n_taps + order : n_taps + 2 * order] * jnp.sqrt(-jnp.expm1(-2.0 * decay))
    return taps, decay, gain, mine[n_taps + 2 * order :]


def local(tokens, in_weight, short_filter, decay_rates, residues, skip_gain, out_weight):
    n_ctx, n_ch = lax.axis_size("ctx"), lax.axis_size("ch")
    rows_here = tokens.shape[0]
    chans = in_weight.shape[2] // n_ch
    taps, decay, gain, skip = own_parameters(short_filter, decay_rates, residues, skip_gain, chans)
    if n_ch == 4 and n_ctx % 2 == 0 and chans % 128 == 0 and rows_here % 64 == 0:
        return mix(project(tokens, in_weight), taps, decay, gain, skip, out_weight)
    everyone = lax.all_gather(tokens, "ctx", axis=0, tiled=True)
    terms = jnp.einsum("rd,dsc->src", everyone, in_weight, preferred_element_type=jnp.float32)
    projected = lax.psum_scatter(terms.astype(jnp.bfloat16), "ch", scatter_dimension=2, tiled=True)
    gated = convolve(projected, taps, decay, gain, skip)
    sent = gated.reshape(n_ctx, rows_here, chans)
    mine = lax.all_to_all(sent, "ctx", split_axis=0, concat_axis=0, tiled=True)
    every = lax.all_gather(mine, "ch", axis=0)
    weight = out_weight.reshape(n_ctx, n_ch, chans, out_weight.shape[1])
    mixed = jnp.einsum("jirc,ijcd->rd", every, weight, preferred_element_type=jnp.float32)
    return mixed.astype(jnp.bfloat16)


def solution(mesh):
    in_specs = (
        P("ctx", "ch"),
        P("ch", None, "ctx"),
        P("ch", None, None),
        P("ch", None),
        P("ch", None),
        P("ch"),
        P(None, "ch"),
    )
    out_specs = P("ctx", "ch")
    return jax.shard_map(local, mesh=mesh, in_specs=in_specs, out_specs=out_specs, check_vma=False)
```

```python
import functools

import jax
import jax.numpy as jnp
from jax import lax
from jax.experimental import pallas as pl
from jax.experimental.pallas import tpu as pltpu
from jax.sharding import PartitionSpec as P

LANES = 8


def conv_kernel(x_ref, taps_ref, decay_ref, gain_ref, skip_ref, out_ref, xs, ps, qs):
    _, length, chans = x_ref.shape
    modes = decay_ref.shape[0]
    reach = taps_ref.shape[1] - 1
    run = length // LANES
    rows = 256 if length % 256 == 0 else length

    def widen(k, _):
        at = pl.ds(pl.multiple_of(k * rows, rows), rows)
        for s in range(3):
            xs[s, at, :] = x_ref[s, at, :].astype(jnp.float32)
        return 0

    lax.fori_loop(0, length // rows, widen, 0)

    def wide(row):
        return jnp.broadcast_to(row, (LANES, chans))

    first = lax.broadcasted_iota(jnp.int32, (LANES, chans), 0) == 0
    rates = [decay_ref[n : n + 1, :] for n in range(modes)]
    a = [wide(jnp.exp(-r)) for r in rates]
    taps = [[wide(taps_ref[s, j : j + 1, :]) for j in range(reach + 1)] for s in range(3)]
    zero = jnp.zeros((LANES, chans), jnp.float32)

    def column(ref, t):
        return ref[pl.ds(t, LANES, stride=run), :]

    before = []
    for s in range(3):
        for j in range(1, reach + 1):
            last = column(xs.at[s], run - j)
            before.append(jnp.where(first, 0.0, pltpu.roll(last, 1, 0)))

    def sweep(t, carry):
        past, states = carry
        feats, now = [], []
        for s in range(3):
            x = column(xs.at[s], t)
            mine = past[s * reach : (s + 1) * reach]
            f = taps[s][0] * x
            for j in range(reach):
                f = f + taps[s][j + 1] * mine[j]
            feats.append(f)
            now += [x] + list(mine[: reach - 1])
        p = (feats[1] * feats[2]).astype(jnp.bfloat16).astype(jnp.float32)
        qs[pl.ds(t, LANES, stride=run), :] = feats[0]
        ps[pl.ds(t, LANES, stride=run), :] = p
        return tuple(now), tuple(a[n] * states[n] + p for n in range(modes))

    _, ends = lax.fori_loop(0, run, sweep, (tuple(before), (zero,) * modes), unroll=2)

    starts = []
    for n in range(modes):
        through = wide(jnp.exp(-rates[n] * float(run)))
        state = zero
        for _ in range(LANES - 1):
            state = jnp.where(first, 0.0, pltpu.roll(through * state + ends[n], 1, 0))
        starts.append(state)

    gain = [wide(gain_ref[n : n + 1, :]) for n in range(modes)]
    skip = wide(skip_ref[...])

    def emit(t, states):
        p = column(ps, t)
        states = tuple(a[n] * states[n] + p for n in range(modes))
        terms = [gain[n] * states[n] for n in range(modes)] + [skip * p]
        while len(terms) > 1:
            terms = [sum(terms[k : k + 2][1:], terms[k]) for k in range(0, len(terms), 2)]
        at = pl.ds(t, LANES, stride=run)
        qs[at, :] = qs[at, :] * terms[0]
        return states

    lax.fori_loop(0, run, emit, tuple(starts), unroll=2)

    def narrow(k, _):
        at = pl.ds(pl.multiple_of(k * rows, rows), rows)
        out_ref[at, :] = qs[at, :].astype(jnp.bfloat16)
        return 0

    lax.fori_loop(0, length // rows, narrow, 0)


def convolve(projected, taps, decay, gain, skip):
    _, length, chans = projected.shape
    return pl.pallas_call(
        conv_kernel,
        out_shape=jax.ShapeDtypeStruct((length, chans), jnp.bfloat16),
        in_specs=[pl.BlockSpec(memory_space=pltpu.VMEM)] * 5,
        out_specs=pl.BlockSpec(memory_space=pltpu.VMEM),
        scratch_shapes=[
            pltpu.VMEM((3, length, chans), jnp.float32),
            pltpu.VMEM((length, chans), jnp.float32),
            pltpu.VMEM((length, chans), jnp.float32),
        ],
        compiler_params=pltpu.CompilerParams(vmem_limit_bytes=60 << 20),
    )(projected, taps, decay, gain, skip)


MESH = pl.DeviceIdType.MESH


def remote(src, dst, send, recv, device):
    return pltpu.make_async_remote_copy(
        src_ref=src, dst_ref=dst, send_sem=send, recv_sem=recv, device_id=device, device_id_type=MESH
    )


def project_kernel(
    n_ctx, cuts, tok_ref, w_hbm, out_ref, held, w, part, near, sums, far,
    w_sem, tok_sem, up_s, down_s, line_r, pair_s, pair_r, near_s, near_r, far_s, far_r,
):
    rows = held.shape[1]
    streams, _, width = w.shape
    chans = width // 4
    line = n_ctx // 2
    ctx, ch = lax.axis_index("ctx"), lax.axis_index("ch")
    z, x = lax.div(ctx, 2), lax.rem(ctx, 2)
    y, core = lax.div(ch, 2), lax.rem(ch, 2)
    near_ch, far_ch = y * 2 + 1 - core, (1 - y) * 2 + core
    has_up, has_down = z + 1 < line, z > 0

    load = pltpu.make_async_copy(w_hbm, w, w_sem)
    load.start()
    own = []
    for q in range(cuts):
        fetch = pltpu.make_async_copy(
            tok_ref.at[pl.ds(q * rows, rows), :], held.at[ctx * cuts + q], tok_sem.at[q]
        )
        fetch.start()
        own.append(fetch)

    barrier = pltpu.get_barrier_semaphore()

    def greet(*device):
        pl.semaphore_signal(barrier, inc=1, device_id=device, device_id_type=MESH)

    greet(z * 2 + 1 - x, ch)
    greet(ctx, near_ch)
    greet(ctx, far_ch)

    @pl.when(has_up)
    def _():
        greet(ctx + 2, ch)

    @pl.when(has_down)
    def _():
        greet(ctx - 2, ch)

    pl.semaphore_wait(barrier, 3 + has_up.astype(jnp.int32) + has_down.astype(jnp.int32))

    def slot(src, side):
        return (lax.div(src, cuts) * 2 + side) * cuts + lax.rem(src, cuts)

    def up_copy(src):
        at = held.at[slot(src, x)]
        return remote(at, at, up_s.at[src], line_r.at[src], (ctx + 2, ch))

    def down_copy(src):
        at = held.at[slot(src, x)]
        return remote(at, at, down_s.at[src], line_r.at[src], (ctx - 2, ch))

    def pair_copy(src, side):
        at = held.at[slot(src, side)]
        return remote(at, at, pair_s.at[src], pair_r.at[src], (z * 2 + 1 - x, ch))

    def near_copy(r):
        return remote(part.at[1 - core, r], near.at[r], near_s.at[r], near_r.at[r], (ctx, near_ch))

    def far_copy(r):
        return remote(sums.at[r], far.at[r], far_s.at[r], far_r.at[r], (ctx, far_ch))

    for q in range(cuts):
        own[q].wait()

        @pl.when(has_up)
        def _():
            up_copy(z * cuts + q).start()

        @pl.when(has_down)
        def _():
            down_copy(z * cuts + q).start()

        pair_copy(z * cuts + q, x).start()

    load.wait()

    def compute(r):
        def stream(s, _):
            for half in range(2):
                acc = jnp.dot(
                    held[r],
                    w[s, :, half * 2 * chans : (half + 1) * 2 * chans],
                    preferred_element_type=jnp.float32,
                ).astype(jnp.bfloat16)
                part[0, r, half, s] = acc[:, :chans]
                part[1, r, half, s] = acc[:, chans:]
            return 0

        lax.fori_loop(0, streams, stream, 0)
        near_copy(r).start()

    def combine(r):
        near_copy(r).wait_recv()
        for s in range(streams):
            both = part[core, r, 1 - y, s].astype(jnp.float32) + near[r, 1 - y, s].astype(jnp.float32)
            sums[r, s] = both.astype(jnp.bfloat16)
        far_copy(r).start()

    late = 2 * cuts - 1

    def place(t):
        s = lax.div(t + cuts, cuts) - 1
        away = lax.div(s + 1, 2)
        sign = 2 * lax.rem(s + 1, 2) - 1
        at = z + away * sign
        return at * cuts + lax.rem(t + cuts, cuts), sign, (t >= 0) & (at >= 0) & (at < line)

    def step(s, _):
        at, sign, valid = place(s)

        @pl.when(valid)
        def _():
            @pl.when(s >= cuts)
            def _():
                up_copy(at).wait_recv()

                @pl.when((sign < 0) & has_up)
                def _():
                    up_copy(at).start()

                @pl.when((sign > 0) & has_down)
                def _():
                    down_copy(at).start()

                pair_copy(at, x).start()

            compute(slot(at, x))

        at1, _, valid1 = place(s - late)

        @pl.when(valid1)
        def _():
            pair_copy(at1, 1 - x).wait_recv()
            compute(slot(at1, 1 - x))

        at3, _, valid3 = place(s - 1)

        @pl.when(valid3)
        def _():
            combine(slot(at3, x))

        at2, _, valid2 = place(s - late - 1)

        @pl.when(valid2)
        def _():
            combine(slot(at2, 1 - x))

        return 0

    lax.fori_loop(0, (2 * line - 1) * cuts + late + 1, step, 0)

    def finish(r, _):
        far_copy(r).wait_recv()
        at = pl.ds(pl.multiple_of(r * rows, rows), rows)
        for s in range(streams):
            total = part[core, r, y, s].astype(jnp.float32) + near[r, y, s].astype(jnp.float32)
            out_ref[s, at, :] = (total + far[r, s].astype(jnp.float32)).astype(jnp.bfloat16)
        return 0

    lax.fori_loop(0, n_ctx * cuts, finish, 0)

    def drain(r, _):
        near_copy(r).wait_send()
        far_copy(r).wait_send()
        return 0

    lax.fori_loop(0, n_ctx * cuts, drain, 0)

    def drain_line(src, _):
        pair_copy(src, x).wait_send()

        @pl.when(has_up & (lax.div(src, cuts) <= z))
        def _():
            up_copy(src).wait_send()

        @pl.when(has_down & (lax.div(src, cuts) >= z))
        def _():
            down_copy(src).wait_send()

        return 0

    lax.fori_loop(0, line * cuts, drain_line, 0)


def project(tokens, in_weight):
    n_ctx = lax.axis_size("ctx")
    cuts = 2
    rows, depth = tokens.shape[0] // cuts, tokens.shape[1]
    slots = n_ctx * cuts
    streams, width = in_weight.shape[1:]
    chans = width // 4
    dma = pltpu.SemaphoreType.DMA
    line = n_ctx // 2
    return pl.pallas_call(
        functools.partial(project_kernel, n_ctx, cuts),
        out_shape=jax.ShapeDtypeStruct((streams, slots * rows, chans), jnp.bfloat16),
        in_specs=[pl.BlockSpec(memory_space=pl.ANY)] * 2,
        out_specs=pl.BlockSpec(memory_space=pltpu.VMEM),
        scratch_shapes=[
            pltpu.VMEM((slots, rows, depth), jnp.bfloat16),
            pltpu.VMEM((streams, depth, width), jnp.bfloat16),
            pltpu.VMEM((2, slots, 2, streams, rows, chans), jnp.bfloat16),
            pltpu.VMEM((slots, 2, streams, rows, chans), jnp.bfloat16),
            pltpu.VMEM((slots, streams, rows, chans), jnp.bfloat16),
            pltpu.VMEM((slots, streams, rows, chans), jnp.bfloat16),
            dma,
            dma((cuts,)),
        ]
        + [dma((line * cuts,))] * 5
        + [dma((slots,))] * 4,
        compiler_params=pltpu.CompilerParams(
            collective_id=0, has_side_effects=True, vmem_limit_bytes=62 << 20
        ),
    )(tokens, jnp.transpose(in_weight, (1, 0, 2)))


def mix_kernel(
    n_ctx, x_ref, taps_ref, decay_ref, gain_ref, skip_ref, w_hbm, out_ref,
    g_ref, xs, ps, qs, entering, blocks, w, acc,
    w_sem, sent_s, sent_r, far_s, far_r, near_s, near_r, relay_s, relay_r,
):
    _, rows, chans = g_ref.shape
    modes = decay_ref.shape[0]
    reach = taps_ref.shape[1] - 1
    run = rows // LANES
    width = 4 * chans
    ctx, ch = lax.axis_index("ctx"), lax.axis_index("ch")
    y, core = lax.div(ch, 2), lax.rem(ch, 2)
    near_ch, far_ch, cross_ch = y * 2 + 1 - core, (1 - y) * 2 + core, (1 - y) * 2 + 1 - core
    load = pltpu.make_async_copy(w_hbm, w, w_sem)
    load.start()

    def lanes(j):
        return pl.ds(pl.multiple_of(j * chans, chans), chans)

    def peer(k):
        return lax.rem(ctx + k, n_ctx)

    barrier = pltpu.get_barrier_semaphore()

    def greet(device):
        pl.semaphore_signal(barrier, inc=1, device_id=device, device_id_type=MESH)

    def greet_peer(k, _):
        greet((peer(k), ch))
        return 0

    lax.fori_loop(1, n_ctx, greet_peer, 0)
    greet((ctx, near_ch))
    greet((ctx, far_ch))
    acc[...] = jnp.zeros_like(acc)

    def wide(row):
        return jnp.broadcast_to(row, (LANES, chans))

    sub = lax.broadcasted_iota(jnp.int32, (LANES, chans), 0)
    zero = jnp.zeros((LANES, chans), jnp.float32)
    rates = [decay_ref[n : n + 1, :] for n in range(modes)]
    a = [wide(jnp.exp(-r)) for r in rates]
    taps = [[wide(taps_ref[s, j : j + 1, :]) for j in range(reach + 1)] for s in range(3)]
    for s in range(3):
        xs[s, 0:8, :] = jnp.zeros((8, chans), jnp.float32)

    def absorb(k, carry):
        base = pl.multiple_of(k * rows, rows)
        for s in range(3):
            xs[s, pl.ds(base + 8, rows), :] = x_ref[s, pl.ds(base, rows), :].astype(jnp.float32)
        before = []
        for s in range(3):
            for j in range(1, reach + 1):
                before.append(xs[s, pl.ds(base + 8 - j, LANES, stride=run), :])

        def sweep(t, inner):
            past, states = inner
            feats, now = [], []
            for s in range(3):
                x = xs[s, pl.ds(base + 8 + t, LANES, stride=run), :]
                mine = past[s * reach : (s + 1) * reach]
                f = taps[s][0] * x
                for j in range(reach):
                    f = f + taps[s][j + 1] * mine[j]
                feats.append(f)
                now += [x] + list(mine[: reach - 1])
            p = (feats[1] * feats[2]).astype(jnp.bfloat16).astype(jnp.float32)
            qs[pl.ds(base + t, LANES, stride=run), :] = feats[0]
            ps[pl.ds(base + t, LANES, stride=run), :] = p
            return tuple(now), tuple(a[n] * states[n] + p for n in range(modes))

        _, ends = lax.fori_loop(0, run, sweep, (tuple(before), (zero,) * modes), unroll=4)
        following = []
        for n in range(modes):
            through = wide(jnp.exp(-rates[n] * float(run)))
            state = jnp.where(sub == 0, carry[n], pltpu.roll(ends[n], 1, 0))
            power, by = through, 1
            while by < LANES:
                state = state + jnp.where(sub >= by, power * pltpu.roll(state, by, 0), 0.0)
                power, by = power * power, by * 2
            entering[k, n] = state
            following.append(pltpu.roll(through * state + ends[n], 1, 0))
        return tuple(following)

    lax.fori_loop(0, n_ctx, absorb, (zero,) * modes)
    pl.semaphore_wait(barrier, n_ctx + 1)
    gain = [wide(gain_ref[n : n + 1, :]) for n in range(modes)]
    skip = wide(skip_ref[...])

    def emit_block(k):
        base = pl.multiple_of(k * rows, rows)

        def emit(t, states):
            at = pl.ds(base + t, LANES, stride=run)
            p = ps[at, :]
            states = tuple(a[n] * states[n] + p for n in range(modes))
            terms = [gain[n] * states[n] for n in range(modes)] + [skip * p]
            while len(terms) > 1:
                terms = [sum(terms[i : i + 2][1:], terms[i]) for i in range(0, len(terms), 2)]
            qs[at, :] = qs[at, :] * terms[0]
            return states

        lax.fori_loop(0, run, emit, tuple(entering[k, n] for n in range(modes)), unroll=4)
        g_ref[k] = qs[pl.ds(base, rows), :].astype(jnp.bfloat16)

    def offset(k):
        odd = lax.rem(k, 2)
        return n_ctx // 2 + (1 - odd) * lax.div(k, 2) - odd * lax.div(k + 1, 2)

    def sent_copy(dest):
        return remote(
            g_ref.at[dest], blocks.at[ctx, :, lanes(ch)], sent_s.at[dest], sent_r.at[ctx], (dest, ch)
        )

    def arrival(src):
        at = blocks.at[src, :, lanes(ch)]
        return remote(at, at, sent_s.at[src], sent_r.at[src], (src, ch))

    def far_copy(src, j):
        at = blocks.at[src, :, lanes(j)]
        return remote(at, at, far_s.at[src], far_r.at[src], (ctx, far_ch))

    def near_copy(src, j):
        at = blocks.at[src, :, lanes(j)]
        return remote(at, at, near_s.at[src], near_r.at[src], (ctx, near_ch))

    def relay_copy(src, j):
        at = blocks.at[src, :, lanes(j)]
        return remote(at, at, relay_s.at[src], relay_r.at[src], (ctx, near_ch))

    def send(k, _):
        dest = peer(offset(k))
        emit_block(dest)

        @pl.when(k < n_ctx - 1)
        def _():
            sent_copy(dest).start()

        return 0

    lax.fori_loop(0, n_ctx, send, 0)
    blocks[ctx, :, lanes(ch)] = g_ref[ctx]

    def source(k):
        own = jnp.where(k == 0, 0, n_ctx - offset(k - 1))
        return lax.rem(ctx + own, n_ctx)

    def step(k, _):
        @pl.when(k < n_ctx)
        def _():
            src = source(k)

            @pl.when(k > 0)
            def _():
                arrival(src).wait_recv()

            far_copy(src, ch).start()
            near_copy(src, ch).start()

        @pl.when((k >= 1) & (k <= n_ctx))
        def _():
            src = source(k - 1)
            far_copy(src, far_ch).wait_recv()
            relay_copy(src, far_ch).start()

        @pl.when(k == 1)
        def _():
            load.wait()

        @pl.when(k >= 2)
        def _():
            src = source(k - 2)
            near_copy(src, near_ch).wait_recv()
            relay_copy(src, cross_ch).wait_recv()
            at = pl.ds(pl.multiple_of(src * width, width), width)
            acc[...] += jnp.dot(blocks[src], w[at, :], preferred_element_type=jnp.float32)

        return 0

    lax.fori_loop(0, n_ctx + 2, step, 0)
    out_ref[...] = acc[...].astype(jnp.bfloat16)

    def drain(k, _):
        src = peer(k)

        @pl.when(k > 0)
        def _():
            sent_copy(src).wait_send()

        far_copy(src, ch).wait_send()
        near_copy(src, ch).wait_send()
        relay_copy(src, far_ch).wait_send()
        return 0

    lax.fori_loop(0, n_ctx, drain, 0)


def mix(projected, taps, decay, gain, skip, out_weight):
    n_ctx = lax.axis_size("ctx")
    streams, length, chans = projected.shape
    rows = length // n_ctx
    dma = pltpu.SemaphoreType.DMA
    return pl.pallas_call(
        functools.partial(mix_kernel, n_ctx),
        out_shape=jax.ShapeDtypeStruct((rows, out_weight.shape[1]), jnp.bfloat16),
        in_specs=[pl.BlockSpec(memory_space=pltpu.VMEM)] * 5 + [pl.BlockSpec(memory_space=pl.ANY)],
        out_specs=pl.BlockSpec(memory_space=pltpu.VMEM),
        scratch_shapes=[
            pltpu.VMEM((n_ctx, rows, chans), jnp.bfloat16),
            pltpu.VMEM((streams, length + 8, chans), jnp.float32),
            pltpu.VMEM((length, chans), jnp.float32),
            pltpu.VMEM((length, chans), jnp.float32),
            pltpu.VMEM((n_ctx, decay.shape[0], LANES, chans), jnp.float32),
            pltpu.VMEM((n_ctx, rows, 4 * chans), jnp.bfloat16),
            pltpu.VMEM(out_weight.shape, jnp.bfloat16),
            pltpu.VMEM((rows, out_weight.shape[1]), jnp.float32),
            dma,
        ]
        + [dma((n_ctx,))] * 8,
        compiler_params=pltpu.CompilerParams(
            collective_id=1, has_side_effects=True, vmem_limit_bytes=62 << 20
        ),
    )(projected, taps, decay, gain, skip, out_weight)


def own_parameters(short_filter, decay_rates, residues, skip_gain, chans):
    n_ctx, n_ch = lax.axis_size("ctx"), lax.axis_size("ch")
    start = lax.axis_index("ctx") * chans
    flat = short_filter.reshape(short_filter.shape[0], -1)
    packed = jnp.concatenate([flat, decay_rates, residues, skip_gain[:, None]], axis=1)
    piece = lax.dynamic_slice_in_dim(packed, start, chans, 0)
    pairs = []
    for s in range(n_ctx):
        for c in range(n_ch):
            pairs.append((s * n_ch + c, c * n_ctx + s))
    mine = lax.ppermute(piece, ("ctx", "ch"), pairs).T
    n_taps, order = flat.shape[1], decay_rates.shape[1]
    taps = mine[:n_taps].reshape(short_filter.shape[1], short_filter.shape[2], chans)
    decay = mine[n_taps : n_taps + order]
    gain = mine[n_taps + order : n_taps + 2 * order] * jnp.sqrt(-jnp.expm1(-2.0 * decay))
    return taps, decay, gain, mine[n_taps + 2 * order :]


def local(tokens, in_weight, short_filter, decay_rates, residues, skip_gain, out_weight):
    n_ctx, n_ch = lax.axis_size("ctx"), lax.axis_size("ch")
    rows_here = tokens.shape[0]
    chans = in_weight.shape[2] // n_ch
    taps, decay, gain, skip = own_parameters(short_filter, decay_rates, residues, skip_gain, chans)
    if n_ch == 4 and n_ctx % 2 == 0 and chans % 128 == 0 and rows_here % 64 == 0:
        return mix(project(tokens, in_weight), taps, decay, gain, skip, out_weight)
    everyone = lax.all_gather(tokens, "ctx", axis=0, tiled=True)
    terms = jnp.einsum("rd,dsc->src", everyone, in_weight, preferred_element_type=jnp.float32)
    projected = lax.psum_scatter(terms.astype(jnp.bfloat16), "ch", scatter_dimension=2, tiled=True)
    gated = convolve(projected, taps, decay, gain, skip)
    sent = gated.reshape(n_ctx, rows_here, chans)
    mine = lax.all_to_all(sent, "ctx", split_axis=0, concat_axis=0, tiled=True)
    every = lax.all_gather(mine, "ch", axis=0)
    weight = out_weight.reshape(n_ctx, n_ch, chans, out_weight.shape[1])
    mixed = jnp.einsum("jirc,ijcd->rd", every, weight, preferred_element_type=jnp.float32)
    return mixed.astype(jnp.bfloat16)


def solution(mesh):
    in_specs = (
        P("ctx", "ch"),
        P("ch", None, "ctx"),
        P("ch", None, None),
        P("ch", None),
        P("ch", None),
        P("ch"),
        P(None, "ch"),
    )
    out_specs = P("ctx", "ch")
    return jax.shard_map(local, mesh=mesh, in_specs=in_specs, out_specs=out_specs, check_vma=False)
```
